32 devices in a mesh: groups: 2 (over y), lon: 4 (over z), lat: 4 (over x, core).
Axes of the slice: x: 2, y: 2, z: 4, core: 2. Of those that a mesh axis runs over, the one named last changes fastest.
Arguments:
- fields: bfloat16 [768, 112, 256], P(('groups', 'lat'), 'lon'), parts along dimension 0, may hold values from -6 to 6
- norm_gains: float32 [3, 256], replicated, may hold values from 0.25 to 1.75
- lon_qkv: bfloat16 [256, 768], replicated, may hold values from -0.375 to 0.375
- lon_out: bfloat16 [256, 256], replicated, may hold values from -0.375 to 0.375
- lat_qkv: bfloat16 [256, 768], replicated, may hold values from -0.375 to 0.375
- lat_out: bfloat16 [256, 256], replicated, may hold values from -0.375 to 0.375
- logit_scales: float32 [2, 8], replicated, may hold values from 0.08 to 7.6
- conv_taps: float32 [25, 256], replicated, may hold values from -1.25 to 1.25
- mlp_in: bfloat16 [256, 2048], replicated, may hold values from -0.375 to 0.375
- mlp_down: bfloat16 [1024, 256], replicated, may hold values from -0.1875 to 0.1875
Outputs:
- mixed_grid: bfloat16 [768, 112, 256], P(('groups', 'lat'), 'lon'), parts along dimension 0
The draws below stay inside these ranges and needn't reach their ends.
There are 2 independent parts, one for each index of `groups`. The reference program is written for one: setup_inputs(seed, part) draws one part's arguments, and reference() takes and returns one part's arrays. A program takes and returns all parts, laid end to end along the dimension named above; an argument that names none is the same for every part. Nothing has to cross between parts.
All inputs are finite; a program needn't handle non-finite values.
Results may differ from the reference program's by a relative error of at most 0.019.
The reference program's roundings to bfloat16 on the way count: a program that leaves them out, or rounds other values in their place, can miss the bound.
Values may be sent and summed in bfloat16 or wider, within the bound.
No kernel may reach another device: no remote copies, remote signals or barrier semaphores. Data moves between devices by JAX's collectives and lax.ppermute only.
A program may use at most 64 MiB of HBM per device.

```python
import math
import jax
import jax.numpy as jnp
from jax import lax

D = 256
HEADS = 8
HD = 32
HID = 1024
KERNEL = 5
NLAT = 384
NLON = 112


def draw_logit_scales(key, part):
    factor = jnp.exp(jax.random.uniform(key, (2, HEADS), jnp.float32, math.log(0.5), math.log(2.0)))
    return (factor * HD ** (-0.5)).astype(jnp.float32)


def level_of(rng, extent, cuts, low, top_value):
    factor_of, own = 1.0, jax.random.fold_in(rng, 6)
    for position, parts in cuts:
        draws = jnp.exp(jax.random.uniform(jax.random.fold_in(own, position), (parts,), jnp.float32, low / len(cuts), top_value / len(cuts)))
        factor_of = factor_of * jnp.repeat(draws, extent[position] // parts).reshape([-1 if axis == position else 1 for axis in range(len(extent))])
    return factor_of


def bell_draw(key, dims, scale, bound, cuts=(), kind=jnp.bfloat16):
    array = scale * jax.random.normal(key, dims, jnp.float32)
    if cuts:
        array = array * level_of(key, dims, cuts, -0.22, 0.18)
    return jnp.clip(array, -bound, bound).astype(kind)


def setup_inputs(seed: int = 0, part: int = 0) -> dict:
    keys = jax.random.split(jax.random.key(seed), 11)
    part_keys = jax.random.split(jax.random.fold_in(keys[10], part), 11)
    return {
        "fields": bell_draw(part_keys[0], (NLAT, NLON, D), 1.0, 6.0, ((0, 4), (1, 4))),
        "norm_gains": jnp.clip(1.0 + 0.15 * jax.random.normal(keys[1], (3, D), jnp.float32), 0.25, 1.75),
        "lon_qkv": bell_draw(keys[2], (D, 3 * D), D ** -0.5, 0.375),
        "lon_out": bell_draw(keys[3], (D, D), D ** -0.5, 0.375),
        "lat_qkv": bell_draw(keys[4], (D, 3 * D), D ** -0.5, 0.375),
        "lat_out": bell_draw(keys[5], (D, D), D ** -0.5, 0.375),
        "logit_scales": draw_logit_scales(jax.random.fold_in(keys[10], 71), part),
        "conv_taps": bell_draw(keys[7], (KERNEL * KERNEL, D), (KERNEL * KERNEL) ** -0.5, 1.25, (), jnp.float32),
        "mlp_in": bell_draw(keys[8], (D, 2 * HID), D ** -0.5, 0.375),
        "mlp_down": bell_draw(keys[9], (HID, D), HID ** -0.5, 0.1875),
    }


EPSILON = 1e-05

def layer_norm(values, gains):
    average = lax.optimization_barrier(jnp.mean(values, -1, keepdims=True))
    centred = values - average
    spread = lax.optimization_barrier(jnp.mean(centred * centred, -1, keepdims=True))
    return centred * lax.rsqrt(spread + EPSILON) * gains

def line_attention(one_line, qkv_weight, out_weight, factors):
    features = one_line.shape[-1]
    heads = factors.shape[0]
    qkv_all = jnp.dot(one_line, qkv_weight, preferred_element_type=jnp.float32).astype(jnp.bfloat16)
    qkv_all = lax.optimization_barrier(qkv_all).astype(jnp.float32)
    queries = qkv_all[:, :features].reshape(-1, heads, features // heads)
    keys_in = qkv_all[:, features:2 * features].reshape(-1, heads, features // heads)
    values_in = qkv_all[:, 2 * features:].reshape(-1, heads, features // heads)
    scores = jnp.einsum('qhd,khd->hqk', queries, keys_in) * factors[:, None, None]
    weights = jnp.exp(scores - lax.optimization_barrier(jnp.max(scores, -1, keepdims=True)))
    totals = lax.optimization_barrier(jnp.sum(weights, -1))
    rounded = lax.optimization_barrier(weights.astype(jnp.bfloat16)).astype(jnp.float32)
    context = jnp.einsum('hqk,khd->qhd', rounded, values_in) / jnp.transpose(totals)[:, :, None]
    context = context.reshape(-1, features).astype(jnp.bfloat16)
    return jnp.dot(context, out_weight, preferred_element_type=jnp.float32).astype(jnp.bfloat16)

def reference(fields, norm_gains, lon_qkv, lon_out, lat_qkv, lat_out, logit_scales, conv_taps, mlp_in, mlp_down):
    anchor = fields.astype(jnp.float32)
    normed = layer_norm(anchor, norm_gains[0]).astype(jnp.bfloat16)
    lon_mix = lax.map(lambda one_line: line_attention(one_line, lon_qkv, lon_out, logit_scales[0]), normed)
    first_state = (anchor + lon_mix.astype(jnp.float32)).astype(jnp.bfloat16)
    first_wide = first_state.astype(jnp.float32)
    normed = layer_norm(first_wide, norm_gains[1]).astype(jnp.bfloat16)
    columns = jnp.swapaxes(normed, 0, 1)
    lat_mix = lax.map(lambda one_line: line_attention(one_line, lat_qkv, lat_out, logit_scales[1]), columns)
    lat_mix = jnp.swapaxes(lat_mix, 0, 1)
    second_state = (first_wide + lat_mix.astype(jnp.float32)).astype(jnp.bfloat16)
    grid_wide = second_state.astype(jnp.float32)
    margin = KERNEL // 2
    padded = jnp.pad(grid_wide, ((margin, margin), (0, 0), (0, 0)))
    padded = jnp.concatenate([padded[:, NLON - margin:], padded, padded[:, :margin]], axis=1)
    smoothed = jnp.zeros((NLAT, NLON, D), jnp.float32)
    for row_tap in range(KERNEL):
        for col_tap in range(KERNEL):
            smoothed = smoothed + conv_taps[row_tap * KERNEL + col_tap] * padded[row_tap:row_tap + NLAT, col_tap:col_tap + NLON]
    normed = layer_norm(smoothed, norm_gains[2]).astype(jnp.bfloat16)
    gate_up = jnp.dot(normed.reshape(-1, D), mlp_in, preferred_element_type=jnp.float32)
    hidden = (jax.nn.silu(gate_up[:, :HID]) * gate_up[:, HID:]).astype(jnp.bfloat16)
    update = jnp.dot(hidden, mlp_down, preferred_element_type=jnp.float32).reshape(NLAT, NLON, D)
    return (grid_wide + update).astype(jnp.bfloat16)
```

```python
import functools

import jax
import jax.numpy as jnp
from jax import lax
from jax.experimental import pallas as pl
from jax.experimental.pallas import tpu as pltpu
from jax.sharding import PartitionSpec as P

KERNEL = 5
MARGIN = KERNEL // 2
EPSILON = 1e-05
LOG2E = 1.4426950408889634
LANES = 128

NT = (((1,), (1,)), ((), ()))
TN = (((0,), (0,)), ((), ()))


def dot(a, b, dims=(((1,), (0,)), ((), ()))):
    return lax.dot_general(a, b, dims, preferred_element_type=jnp.float32)


def padded(n, unit):
    return -(-n // unit) * unit


def layer_norm(values, gains):
    average = jnp.mean(values, -1, keepdims=True)
    centred = values - average
    spread = jnp.mean(centred * centred, -1, keepdims=True)
    return centred * lax.rsqrt(spread + EPSILON) * gains


def attend_line(keys, queries_t, values_t, factors, diag, out_w, count, heads):
    size = queries_t.shape[0] // heads
    width = queries_t.shape[1]
    parts = []
    for h in range(heads):
        rows = slice(h * size, (h + 1) * size)
        diag[h, rows, :] = queries_t[rows]
        scores = dot(keys, diag[h])[:count]
        top = jnp.max(scores, 0, keepdims=True)
        weights = jnp.exp2((scores - top) * factors[h])
        total = jnp.sum(weights, 0, keepdims=True)
        rounded = weights.astype(jnp.bfloat16)
        if width > count:
            rounded = jnp.concatenate([rounded, jnp.zeros((width - count, width), jnp.bfloat16)], 0)
        parts.append((dot(values_t[rows], rounded) / total).astype(jnp.bfloat16))
    return dot(jnp.concatenate(parts, 0), out_w, TN)


def lon_kernel(factor_ref, x_ref, gain_ref, wk_ref, wqv_ref, wo_ref, o_ref, state, normed, diag, *, bands, blocks, count):
    cols, rows, features = x_ref.shape
    heads = diag.shape[0]
    width = diag.shape[2]
    diag[...] = jnp.zeros_like(diag)
    step = cols // bands
    lanes = [slice(c, c + LANES) for c in range(0, features, LANES)]

    @pl.loop(0, bands)
    def _(i):
        x = x_ref[pl.ds(i * step, step)].astype(jnp.float32).reshape(step * rows, features)
        y = layer_norm(x, gain_ref[...])
        at = pl.ds(pl.multiple_of(i * step * rows, 8), step * rows)
        for c, part in enumerate(lanes):
            state[c, at, :] = x[:, part]
            normed[c, at, :] = y[:, part]

    factors = [factor_ref[h] for h in range(heads)]

    @pl.loop(0, count)
    def _(r):
        at = pl.ds(r, cols, stride=rows)
        line = [normed.at[c][at, :].astype(jnp.bfloat16) for c in range(len(lanes))]
        line = jnp.concatenate(line, 1)
        if width > cols:
            line = jnp.concatenate([line, jnp.zeros((width - cols, features), jnp.bfloat16)], 0)
        keys = dot(line, wk_ref[...]).astype(jnp.bfloat16)
        both = dot(wqv_ref[...], line, NT).astype(jnp.bfloat16)
        mix = attend_line(keys, both[:features], both[features:], factors, diag, wo_ref[...], cols, heads)
        mix = mix[:cols].astype(jnp.bfloat16).astype(jnp.float32)
        for c, part in enumerate(lanes):
            state.at[c][at, :] = state.at[c][at, :] + mix[:, part]

    size = o_ref.shape[1]
    for i in range(bands):
        for j in range(blocks):
            at = slice((j * bands + i) * size * rows, (j * bands + i + 1) * size * rows)
            y = jnp.concatenate([state[c, at, :] for c in range(len(lanes))], 1)
            o_ref[i * blocks + j] = y.reshape(size, rows, features).astype(jnp.bfloat16)


def lat_kernel(factor_ref, x_ref, gain_ref, wk_ref, wqv_ref, wo_ref, o_ref, state, diag, *, bands):
    sources, _, rows, features = x_ref.shape
    length = sources * rows
    heads = diag.shape[0]

    @pl.when(pl.program_id(0) == 0)
    def _():
        diag[...] = jnp.zeros_like(diag)
        state[...] = jnp.zeros_like(state)

    x = x_ref[:, 0].astype(jnp.float32).reshape(length, features)
    line = layer_norm(x, gain_ref[...]).astype(jnp.bfloat16)
    keys = dot(line, wk_ref[...]).astype(jnp.bfloat16)
    both = dot(wqv_ref[...], line, NT).astype(jnp.bfloat16)
    factors = [factor_ref[h] for h in range(heads)]
    mix = attend_line(keys, both[:features], both[features:], factors, diag, wo_ref[...], length, heads)
    state[8 : 8 + length, :] = x + mix.astype(jnp.bfloat16).astype(jnp.float32)
    band = length // bands
    for i in range(bands):
        first = 8 + i * band - MARGIN
        o_ref[i, 0] = state[first : first + band + 2 * MARGIN, :].astype(jnp.bfloat16)


def mixer_kernel(s_ref, before_ref, after_ref, taps_ref, gain_ref, win_ref, wdown_ref, o_ref, wide, normed):
    cols, tall, features = s_ref.shape
    rows = tall - 2 * MARGIN
    step = o_ref.shape[0]
    hidden_len = wdown_ref.shape[0]
    g = pl.program_id(0)

    @pl.when(g == 0)
    def _():
        wide[:MARGIN, :tall] = before_ref[...].astype(jnp.float32)
        wide[MARGIN + cols :, :tall] = after_ref[...].astype(jnp.float32)
        wide[MARGIN : MARGIN + cols, :tall] = s_ref[...].astype(jnp.float32)

    for c in range(step):
        total = None
        for dy in range(KERNEL):
            part = None
            for dx in range(KERNEL):
                tap = taps_ref[dy * KERNEL + dx : dy * KERNEL + dx + 1, :]
                term = wide[g * step + c + dx, dy : dy + rows, :] * tap
                part = term if part is None else part + term
            total = part if total is None else total + part
        normed[c * rows : (c + 1) * rows, :] = layer_norm(total, gain_ref[...]).astype(jnp.bfloat16)

    for c in range(step):
        line = normed[c * rows : (c + 1) * rows, :]
        gate = dot(line, win_ref[:, :hidden_len])
        up = dot(line, win_ref[:, hidden_len:])
        hidden = (0.5 * gate * (1.0 + jnp.tanh(0.5 * gate)) * up).astype(jnp.bfloat16)
        update = dot(hidden, wdown_ref[...])
        kept = wide[g * step + c + MARGIN, MARGIN : MARGIN + rows, :]
        o_ref[c] = (kept + update).astype(jnp.bfloat16)


def whole(shape):
    return pl.BlockSpec(shape, lambda *_: (0,) * len(shape))


def split_weights(qkv, features):
    keys = qkv[:, features : 2 * features]
    both = jnp.concatenate([qkv[:, :features], qkv[:, 2 * features :]], 1).T
    return keys, both


def per_device(
    fields,
    norm_gains,
    lon_qkv,
    lon_out,
    lat_qkv,
    lat_out,
    logit_scales,
    conv_taps,
    mlp_in,
    mlp_down,
):
    lat_rows, lon_cols, features = fields.shape
    heads = logit_scales.shape[1]
    blocks = lax.axis_size("lon")
    bands = lax.axis_size("lat")
    sub_rows = lat_rows // blocks
    sub_cols = lon_cols // bands
    all_cols = lon_cols * blocks
    all_rows = lat_rows * bands
    factors = logit_scales * LOG2E
    smem = pl.BlockSpec(memory_space=pltpu.SMEM)
    bf16, f32 = jnp.bfloat16, jnp.float32

    stacked = jnp.transpose(fields.reshape(blocks, sub_rows, lon_cols, features), (0, 2, 1, 3))
    tall_rows = padded(sub_rows, 8)
    if tall_rows > sub_rows:
        stacked = jnp.pad(stacked, ((0, 0), (0, 0), (0, tall_rows - sub_rows), (0, 0)))
    lines = lax.all_to_all(stacked, "lon", split_axis=0, concat_axis=0, tiled=True)
    lines = lines.reshape(all_cols, tall_rows, features)
    wk, wqv = split_weights(lon_qkv, features)
    width = padded(all_cols, LANES)
    first_state = pl.pallas_call(
        functools.partial(lon_kernel, bands=bands, blocks=blocks, count=sub_rows),
        out_shape=jax.ShapeDtypeStruct((bands * blocks, sub_cols, tall_rows, features), bf16),
        in_specs=[smem] + [pl.BlockSpec(memory_space=pltpu.VMEM)] * 5,
        out_specs=pl.BlockSpec(memory_space=pltpu.VMEM),
        scratch_shapes=[
            pltpu.VMEM((features // LANES, all_cols * tall_rows, LANES), f32),
            pltpu.VMEM((features // LANES, all_cols * tall_rows, LANES), f32),
            pltpu.VMEM((heads, features, width), bf16),
        ],
        name="lon_attention",
    )(factors[0], lines, norm_gains[0:1], wk, wqv, lon_out)

    columns = lax.all_to_all(first_state, ("lat", "lon"), split_axis=0, concat_axis=0, tiled=True)
    if tall_rows > sub_rows:
        columns = jnp.swapaxes(columns[:, :, :sub_rows], 0, 1).reshape(1, sub_cols, all_rows, features)
    wk, wqv = split_weights(lat_qkv, features)
    tall = lat_rows + 2 * MARGIN
    second = pl.pallas_call(
        functools.partial(lat_kernel, bands=bands),
        grid=(sub_cols,),
        out_shape=jax.ShapeDtypeStruct((bands, sub_cols, tall, features), bf16),
        in_specs=[
            smem,
            pl.BlockSpec((columns.shape[0], 1, columns.shape[2], features), lambda k: (0, k, 0, 0)),
            whole((1, features)),
            whole((features, features)),
            whole((2 * features, features)),
            whole((features, features)),
        ],
        out_specs=pl.BlockSpec((bands, 1, tall, features), lambda k: (0, k, 0, 0)),
        scratch_shapes=[
            pltpu.VMEM((all_rows + 16, features), f32),
            pltpu.VMEM((heads, features, all_rows), bf16),
        ],
        name="lat_attention",
    )(factors[1], columns, norm_gains[1:2], wk, wqv, lat_out)

    block = lax.all_to_all(second, "lat", split_axis=0, concat_axis=0, tiled=True)
    block = block.reshape(lon_cols, tall, features)
    up = [(i, (i + 1) % blocks) for i in range(blocks)]
    before = lax.ppermute(block[lon_cols - MARGIN :], "lon", up)
    after = lax.ppermute(block[:MARGIN], "lon", [(j, i) for i, j in up])
    steps = bands
    mixed = pl.pallas_call(
        mixer_kernel,
        grid=(steps,),
        out_shape=jax.ShapeDtypeStruct((lon_cols, lat_rows, features), bf16),
        in_specs=[
            whole((lon_cols, tall, features)),
            whole((MARGIN, tall, features)),
            whole((MARGIN, tall, features)),
            whole(conv_taps.shape),
            whole((1, features)),
            whole(mlp_in.shape),
            whole(mlp_down.shape),
        ],
        out_specs=pl.BlockSpec((lon_cols // steps, lat_rows, features), lambda g: (g, 0, 0)),
        scratch_shapes=[
            pltpu.VMEM((lon_cols + 2 * MARGIN, padded(tall, 8), features), f32),
            pltpu.VMEM((lon_cols // steps * lat_rows, features), bf16),
        ],
        name="mixer",
    )(block, before, after, conv_taps, norm_gains[2:3], mlp_in, mlp_down)
    return jnp.transpose(mixed, (1, 0, 2))


def solution(mesh):
    in_specs = (P(("groups", "lat"), "lon", None), P(), P(), P(), P(), P(), P(), P(), P(), P())
    out_specs = P(("groups", "lat"), "lon", None)
    return jax.shard_map(
        per_device, mesh=mesh, in_specs=in_specs, out_specs=out_specs, check_vma=False
    )
```

```python
import functools

import jax
import jax.numpy as jnp
from jax import lax
from jax.experimental import pallas as pl
from jax.experimental.pallas import tpu as pltpu
from jax.sharding import PartitionSpec as P

KERNEL = 5
MARGIN = KERNEL // 2
EPSILON = 1e-05
LOG2E = 1.4426950408889634
LANES = 128

NT = (((1,), (1,)), ((), ()))
TN = (((0,), (0,)), ((), ()))


def dot(a, b, dims=(((1,), (0,)), ((), ()))):
    return lax.dot_general(a, b, dims, preferred_element_type=jnp.float32)


def padded(n, unit):
    return -(-n // unit) * unit


def layer_norm(values, gains):
    average = jnp.mean(values, -1, keepdims=True)
    centred = values - average
    spread = jnp.mean(centred * centred, -1, keepdims=True)
    return centred * lax.rsqrt(spread + EPSILON) * gains


def attend_line(keys, both, factors, diag, out_w, group):
    features = keys.shape[1]
    heads = len(factors)
    size = features // heads
    parts = [None] * heads
    for h in range(heads):
        rows = slice(h * size, (h + 1) * size)
        diag[h, rows, :] = both[rows]
    for start in range(0, heads, group):
        some = range(start, start + group)
        scores = {h: dot(keys, diag[h]) for h in some}
        rounded, total = {}, {}
        for h in some:
            top = jnp.max(scores[h], 0, keepdims=True)
            weights = jnp.exp2((scores[h] - top) * factors[h])
            total[h] = jnp.sum(weights, 0, keepdims=True)
            rounded[h] = weights.astype(jnp.bfloat16)
        for h in some:
            values = both[features + h * size : features + (h + 1) * size]
            parts[h] = (dot(values, rounded[h]) / total[h]).astype(jnp.bfloat16)
    return dot(jnp.concatenate(parts, 0), out_w, TN)


def attend_lines(keys, both, factors, diag, out_w, count, width, heads, lines):
    features = keys.shape[1]
    size = features // heads
    pairs = [(u, h) for u in range(lines) for h in range(heads)]
    parts = {}
    scores = {}
    for u, h in pairs:
        rows = slice(h * size, (h + 1) * size)
        diag[u * heads + h, rows, :] = both[rows, u * width : (u + 1) * width]
    for u, h in pairs:
        scores[u, h] = dot(keys[u * width : u * width + count], diag[u * heads + h])
    rounded, total = {}, {}
    for u, h in pairs:
        top = jnp.max(scores[u, h], 0, keepdims=True)
        weights = jnp.exp2((scores[u, h] - top) * factors[h])
        total[u, h] = jnp.sum(weights, 0, keepdims=True)
        packed = weights.astype(jnp.bfloat16)
        if width > count:
            packed = jnp.concatenate([packed, jnp.zeros((width - count, width), jnp.bfloat16)], 0)
        rounded[u, h] = packed
    for u, h in pairs:
        values = both[features + h * size : features + (h + 1) * size, u * width : (u + 1) * width]
        parts[u, h] = (dot(values, rounded[u, h]) / total[u, h]).astype(jnp.bfloat16)
    context = [jnp.concatenate([parts[u, h] for h in range(heads)], 0) for u in range(lines)]
    return dot(jnp.concatenate(context, 1), out_w, TN)


def lon_kernel(factor_ref, x_ref, gain_ref, wk_ref, wqv_ref, wo_ref, o_ref, state, normed, diag, *, bands, blocks, count):
    cols, rows, features = x_ref.shape
    heads = factor_ref.shape[0]
    width = diag.shape[2]
    diag[...] = jnp.zeros_like(diag)
    step = cols // bands
    lanes = [slice(c, c + LANES) for c in range(0, features, LANES)]

    @pl.loop(0, bands)
    def _(i):
        x = x_ref[pl.ds(i * step, step)].astype(jnp.float32).reshape(step * rows, features)
        y = layer_norm(x, gain_ref[...])
        at = pl.ds(pl.multiple_of(i * step * rows, 8), step * rows)
        for c, part in enumerate(lanes):
            state[c, at, :] = x[:, part]
            normed[c, at, :] = y[:, part]

    factors = [factor_ref[h] for h in range(heads)]

    unroll = diag.shape[0] // heads

    @pl.loop(0, count // unroll)
    def _(group):
        spots = [pl.ds(group * unroll + u, cols, stride=rows) for u in range(unroll)]
        lines = []
        for at in spots:
            line = [normed.at[c][at, :].astype(jnp.bfloat16) for c in range(len(lanes))]
            line = jnp.concatenate(line, 1)
            if width > cols:
                line = jnp.concatenate([line, jnp.zeros((width - cols, features), jnp.bfloat16)], 0)
            lines.append(line)
        stack = jnp.concatenate(lines, 0)
        keys = dot(stack, wk_ref[...]).astype(jnp.bfloat16)
        both = dot(wqv_ref[...], stack, NT).astype(jnp.bfloat16)
        mixes = attend_lines(keys, both, factors, diag, wo_ref[...], cols, width, heads, unroll)
        for u, at in enumerate(spots):
            mix = mixes[u * width : u * width + cols].astype(jnp.bfloat16).astype(jnp.float32)
            for c, part in enumerate(lanes):
                state.at[c][at, :] = state.at[c][at, :] + mix[:, part]

    size = o_ref.shape[1]
    for i in range(bands):
        for j in range(blocks):
            at = slice((j * bands + i) * size * rows, (j * bands + i + 1) * size * rows)
            y = jnp.concatenate([state[c, at, :] for c in range(len(lanes))], 1)
            o_ref[i * blocks + j] = y.reshape(size, rows, features).astype(jnp.bfloat16)


def lat_kernel(factor_ref, x_ref, gain_ref, wk_ref, wqv_ref, wo_ref, o_ref, state, diag, *, bands):
    sources, _, rows, features = x_ref.shape
    length = sources * rows
    heads = diag.shape[0]

    @pl.when(pl.program_id(0) == 0)
    def _():
        diag[...] = jnp.zeros_like(diag)
        state[...] = jnp.zeros_like(state)

    x = x_ref[:, 0].astype(jnp.float32).reshape(length, features)
    line = layer_norm(x, gain_ref[...]).astype(jnp.bfloat16)
    keys = dot(line, wk_ref[...]).astype(jnp.bfloat16)
    both = dot(wqv_ref[...], line, NT).astype(jnp.bfloat16)
    factors = [factor_ref[h] for h in range(heads)]
    mix = attend_line(keys, both, factors, diag, wo_ref[...], 8)
    state[8 : 8 + length, :] = x + mix.astype(jnp.bfloat16).astype(jnp.float32)
    band = length // bands
    for i in range(bands):
        first = 8 + i * band - MARGIN
        o_ref[i, 0] = state[first : first + band + 2 * MARGIN, :].astype(jnp.bfloat16)


def mixer_kernel(s_ref, before_ref, after_ref, taps_ref, gain_ref, win_ref, wdown_ref, o_ref, wide, normed):
    cols, tall, features = s_ref.shape
    rows = tall - 2 * MARGIN
    step = o_ref.shape[0]
    hidden_len = wdown_ref.shape[0]
    g = pl.program_id(0)

    @pl.when(g == 0)
    def _():
        wide[:MARGIN, :tall] = before_ref[...].astype(jnp.float32)
        wide[MARGIN + cols :, :tall] = after_ref[...].astype(jnp.float32)
        wide[MARGIN : MARGIN + cols, :tall] = s_ref[...].astype(jnp.float32)

    for c in range(step):
        total = None
        for dy in range(KERNEL):
            part = None
            for dx in range(KERNEL):
                tap = taps_ref[dy * KERNEL + dx : dy * KERNEL + dx + 1, :]
                term = wide[g * step + c + dx, dy : dy + rows, :] * tap
                part = term if part is None else part + term
            total = part if total is None else total + part
        normed[c * rows : (c + 1) * rows, :] = layer_norm(total, gain_ref[...]).astype(jnp.bfloat16)

    for c in range(step):
        line = normed[c * rows : (c + 1) * rows, :]
        gate = dot(line, win_ref[:, :hidden_len])
        up = dot(line, win_ref[:, hidden_len:])
        hidden = (0.5 * gate * (1.0 + jnp.tanh(0.5 * gate)) * up).astype(jnp.bfloat16)
        update = dot(hidden, wdown_ref[...])
        kept = wide[g * step + c + MARGIN, MARGIN : MARGIN + rows, :]
        o_ref[c] = (kept + update).astype(jnp.bfloat16)


def whole(shape):
    return pl.BlockSpec(shape, lambda *_: (0,) * len(shape))


def split_weights(qkv, features):
    keys = qkv[:, features : 2 * features]
    both = jnp.concatenate([qkv[:, :features], qkv[:, 2 * features :]], 1).T
    return keys, both


SMEM = pl.BlockSpec(memory_space=pltpu.SMEM)
VMEM = pl.BlockSpec(memory_space=pltpu.VMEM)


def lon_call(lines, factors, gains, qkv, out_w, bands, blocks, count):
    all_cols, rows, features = lines.shape
    heads = factors.shape[0]
    wk, wqv = split_weights(qkv, features)
    unroll = next(u for u in (8, 2, 1) if u == 1 or (count % u == 0 and all_cols <= 2 * LANES))
    return pl.pallas_call(
        functools.partial(lon_kernel, bands=bands, blocks=blocks, count=count),
        out_shape=jax.ShapeDtypeStruct(
            (bands * blocks, all_cols // (bands * blocks), rows, features), jnp.bfloat16
        ),
        in_specs=[SMEM] + [VMEM] * 5,
        out_specs=VMEM,
        scratch_shapes=[
            pltpu.VMEM((features // LANES, all_cols * rows, LANES), jnp.float32),
            pltpu.VMEM((features // LANES, all_cols * rows, LANES), jnp.float32),
            pltpu.VMEM((heads * unroll, features, padded(all_cols, LANES)), jnp.bfloat16),
        ],
        name="lon_attention",
    )(factors, lines, gains, wk, wqv, out_w)


def lat_call(columns, factors, gains, qkv, out_w, bands):
    sources, count, rows, features = columns.shape
    heads = factors.shape[0]
    length = sources * rows
    tall = length // bands + 2 * MARGIN
    wk, wqv = split_weights(qkv, features)
    return pl.pallas_call(
        functools.partial(lat_kernel, bands=bands),
        grid=(count,),
        out_shape=jax.ShapeDtypeStruct((bands, count, tall, features), jnp.bfloat16),
        in_specs=[
            SMEM,
            pl.BlockSpec((sources, 1, rows, features), lambda k: (0, k, 0, 0)),
            whole((1, features)),
            whole((features, features)),
            whole((2 * features, features)),
            whole((features, features)),
        ],
        out_specs=pl.BlockSpec((bands, 1, tall, features), lambda k: (0, k, 0, 0)),
        scratch_shapes=[
            pltpu.VMEM((length + 16, features), jnp.float32),
            pltpu.VMEM((heads, features, length), jnp.bfloat16),
        ],
        name="lat_attention",
    )(factors, columns, gains, wk, wqv, out_w)


def mixer_call(block, before, after, taps, gains, win, wdown, steps):
    cols, tall, features = block.shape
    rows = tall - 2 * MARGIN
    return pl.pallas_call(
        mixer_kernel,
        grid=(steps,),
        out_shape=jax.ShapeDtypeStruct((cols, rows, features), jnp.bfloat16),
        in_specs=[
            whole(block.shape),
            whole(before.shape),
            whole(after.shape),
            whole(taps.shape),
            whole(gains.shape),
            whole(win.shape),
            whole(wdown.shape),
        ],
        out_specs=pl.BlockSpec((cols // steps, rows, features), lambda g: (g, 0, 0)),
        scratch_shapes=[
            pltpu.VMEM((cols + 2 * MARGIN, padded(tall, 8), features), jnp.float32),
            pltpu.VMEM((cols // steps * rows, features), jnp.bfloat16),
        ],
        name="mixer",
    )(block, before, after, taps, gains, win, wdown)


def per_device(
    fields,
    norm_gains,
    lon_qkv,
    lon_out,
    lat_qkv,
    lat_out,
    logit_scales,
    conv_taps,
    mlp_in,
    mlp_down,
):
    lat_rows, lon_cols, features = fields.shape
    blocks = lax.axis_size("lon")
    bands = lax.axis_size("lat")
    sub_rows = lat_rows // blocks
    tall_rows = padded(sub_rows, 8)
    sub_cols = lon_cols // bands
    all_cols = lon_cols * blocks
    all_rows = lat_rows * bands
    tall = lat_rows + 2 * MARGIN
    factors = logit_scales * LOG2E

    stacked = jnp.transpose(fields.reshape(blocks, sub_rows, lon_cols, features), (0, 2, 1, 3))
    if tall_rows > sub_rows:
        stacked = jnp.pad(stacked, ((0, 0), (0, 0), (0, tall_rows - sub_rows), (0, 0)))
    lines = lax.all_to_all(stacked, "lon", split_axis=0, concat_axis=0, tiled=True)
    lines = lines.reshape(all_cols, tall_rows, features)
    first_state = lon_call(
        lines, factors[0], norm_gains[0:1], lon_qkv, lon_out, bands, blocks, sub_rows
    )

    columns = lax.all_to_all(first_state, ("lat", "lon"), split_axis=0, concat_axis=0, tiled=True)
    if tall_rows > sub_rows:
        columns = jnp.swapaxes(columns[:, :, :sub_rows], 0, 1).reshape(1, sub_cols, all_rows, features)
    second = lat_call(columns, factors[1], norm_gains[1:2], lat_qkv, lat_out, bands)

    block = lax.all_to_all(second, "lat", split_axis=0, concat_axis=0, tiled=True)
    block = block.reshape(lon_cols, tall, features)
    up = [(i, (i + 1) % blocks) for i in range(blocks)]
    before = lax.ppermute(block[lon_cols - MARGIN :], "lon", up)
    after = lax.ppermute(block[:MARGIN], "lon", [(j, i) for i, j in up])
    mixed = mixer_call(block, before, after, conv_taps, norm_gains[2:3], mlp_in, mlp_down, bands)
    return jnp.transpose(mixed, (1, 0, 2))


def solution(mesh):
    in_specs = (P(("groups", "lat"), "lon", None), P(), P(), P(), P(), P(), P(), P(), P(), P())
    out_specs = P(("groups", "lat"), "lon", None)
    return jax.shard_map(
        per_device, mesh=mesh, in_specs=in_specs, out_specs=out_specs, check_vma=False
    )
```

```python
import functools

import jax
import jax.numpy as jnp
from jax import lax
from jax.experimental import pallas as pl
from jax.experimental.pallas import tpu as pltpu
from jax.sharding import PartitionSpec as P

KERNEL = 5
MARGIN = KERNEL // 2
EPSILON = 1e-05
LOG2E = 1.4426950408889634
LANES = 128

NT = (((1,), (1,)), ((), ()))
TN = (((0,), (0,)), ((), ()))


def dot(a, b, dims=(((1,), (0,)), ((), ()))):
    return lax.dot_general(a, b, dims, preferred_element_type=jnp.float32)


def padded(n, unit):
    return -(-n // unit) * unit


def layer_norm(values, gains):
    average = jnp.mean(values, -1, keepdims=True)
    centred = values - average
    spread = jnp.mean(centred * centred, -1, keepdims=True)
    return centred * lax.rsqrt(spread + EPSILON) * gains


def attend_line(keys, both, factors, diag, out_w, group):
    features = keys.shape[1]
    heads = len(factors)
    size = features // heads
    parts = [None] * heads
    for h in range(heads):
        rows = slice(h * size, (h + 1) * size)
        diag[h, rows, :] = both[rows]
    for start in range(0, heads, group):
        some = range(start, start + group)
        scores = {h: dot(keys, diag[h]) for h in some}
        rounded, total = {}, {}
        for h in some:
            top = jnp.max(scores[h], 0, keepdims=True)
            weights = jnp.exp2((scores[h] - top) * factors[h])
            total[h] = jnp.sum(weights, 0, keepdims=True)
            rounded[h] = weights.astype(jnp.bfloat16)
        for h in some:
            values = both[features + h * size : features + (h + 1) * size]
            parts[h] = (dot(values, rounded[h]) / total[h]).astype(jnp.bfloat16)
    return dot(jnp.concatenate(parts, 0), out_w, TN)


def attend_lines(keys, both, factors, diag, out_w, count, width, heads, lines):
    features = keys.shape[1]
    size = features // heads
    pairs = [(u, h) for u in range(lines) for h in range(heads)]
    parts = {}
    scores = {}
    for u, h in pairs:
        rows = slice(h * size, (h + 1) * size)
        diag[u * heads + h, rows, :] = both[rows, u * width : (u + 1) * width]
    for u, h in pairs:
        scores[u, h] = dot(keys[u * width : u * width + count], diag[u * heads + h])
    rounded, total = {}, {}
    for u, h in pairs:
        top = jnp.max(scores[u, h], 0, keepdims=True)
        weights = jnp.exp2((scores[u, h] - top) * factors[h])
        total[u, h] = jnp.sum(weights, 0, keepdims=True)
        packed = weights.astype(jnp.bfloat16)
        if width > count:
            packed = jnp.concatenate([packed, jnp.zeros((width - count, width), jnp.bfloat16)], 0)
        rounded[u, h] = packed
    for u, h in pairs:
        values = both[features + h * size : features + (h + 1) * size, u * width : (u + 1) * width]
        parts[u, h] = (dot(values, rounded[u, h]) / total[u, h]).astype(jnp.bfloat16)
    context = [jnp.concatenate([parts[u, h] for h in range(heads)], 0) for u in range(lines)]
    return dot(jnp.concatenate(context, 1), out_w, TN)


def lon_kernel(factor_ref, x_ref, gain_ref, wk_ref, wqv_ref, wo_ref, *rest, bands, blocks, count):
    *o_refs, state, normed, diag = rest
    cols, rows, features = x_ref.shape
    heads = factor_ref.shape[0]
    width = diag.shape[2]
    diag[...] = jnp.zeros_like(diag)
    step = cols // bands
    lanes = [slice(c, c + LANES) for c in range(0, features, LANES)]

    @pl.loop(0, bands)
    def _(i):
        x = x_ref[pl.ds(i * step, step)].astype(jnp.float32).reshape(step * rows, features)
        y = layer_norm(x, gain_ref[...])
        at = pl.ds(pl.multiple_of(i * step * rows, 8), step * rows)
        for c, part in enumerate(lanes):
            state[c, at, :] = x[:, part]
            normed[c, at, :] = y[:, part]

    factors = [factor_ref[h] for h in range(heads)]

    unroll = diag.shape[0] // heads

    @pl.loop(0, count // unroll)
    def _(group):
        spots = [pl.ds(group * unroll + u, cols, stride=rows) for u in range(unroll)]
        lines = []
        for at in spots:
            line = [normed.at[c][at, :].astype(jnp.bfloat16) for c in range(len(lanes))]
            line = jnp.concatenate(line, 1)
            if width > cols:
                line = jnp.concatenate([line, jnp.zeros((width - cols, features), jnp.bfloat16)], 0)
            lines.append(line)
        stack = jnp.concatenate(lines, 0)
        keys = dot(stack, wk_ref[...]).astype(jnp.bfloat16)
        both = dot(wqv_ref[...], stack, NT).astype(jnp.bfloat16)
        mixes = attend_lines(keys, both, factors, diag, wo_ref[...], cols, width, heads, unroll)
        for u, at in enumerate(spots):
            mix = mixes[u * width : u * width + cols].astype(jnp.bfloat16).astype(jnp.float32)
            for c, part in enumerate(lanes):
                state.at[c][at, :] = state.at[c][at, :] + mix[:, part]

    first = 0
    for o_ref in o_refs:
        size = o_ref.shape[1]
        for i in range(bands):
            for j in range(blocks):
                start = (j * (cols // blocks) + first + i * size) * rows
                at = slice(start, start + size * rows)
                y = jnp.concatenate([state[c, at, :] for c in range(len(lanes))], 1)
                o_ref[i * blocks + j] = y.reshape(size, rows, features).astype(jnp.bfloat16)
        first += bands * size


def lat_kernel(factor_ref, x_ref, gain_ref, wk_ref, wqv_ref, wo_ref, o_ref, state, diag, *, bands):
    sources, _, rows, features = x_ref.shape
    length = sources * rows
    heads = diag.shape[0]

    @pl.when(pl.program_id(0) == 0)
    def _():
        diag[...] = jnp.zeros_like(diag)
        state[...] = jnp.zeros_like(state)

    x = x_ref[:, 0].astype(jnp.float32).reshape(length, features)
    line = layer_norm(x, gain_ref[...]).astype(jnp.bfloat16)
    keys = dot(line, wk_ref[...]).astype(jnp.bfloat16)
    both = dot(wqv_ref[...], line, NT).astype(jnp.bfloat16)
    factors = [factor_ref[h] for h in range(heads)]
    mix = attend_line(keys, both, factors, diag, wo_ref[...], 8)
    state[8 : 8 + length, :] = x + mix.astype(jnp.bfloat16).astype(jnp.float32)
    band = length // bands
    for i in range(bands):
        first = 8 + i * band - MARGIN
        o_ref[i, 0] = state[first : first + band + 2 * MARGIN, :].astype(jnp.bfloat16)


def mixer_kernel(*refs, strips, filled, tile):
    count = 1 + max(piece[0] for _, pieces in strips for piece in pieces)
    inputs = refs[:count]
    taps_ref, gain_ref, win_ref, wdown_ref = refs[count : count + 4]
    o_ref, wide, normed, done, sems = refs[count + 4 + filled :]
    tall, features = inputs[0].shape[1:]
    rows = tall - 2 * MARGIN
    hidden_len = wdown_ref.shape[0]
    outs, at = [], 0
    for first, pieces in strips:
        start = at
        for index, low, high in pieces:
            wide[at : at + high - low, :tall] = inputs[index][low:high].astype(jnp.float32)
            at += high - low
        outs += [(start + c, first + c) for c in range(at - start - 2 * MARGIN)]

    def smooth(n):
        source = outs[n][0]
        total = None
        for dy in range(KERNEL):
            part = None
            for dx in range(KERNEL):
                tap = taps_ref[dy * KERNEL + dx : dy * KERNEL + dx + 1, :]
                term = wide[source + dx] * tap
                part = term if part is None else part + term
            part = part[dy : dy + rows]
            total = part if total is None else total + part
        normed[n * rows : (n + 1) * rows, :] = layer_norm(total, gain_ref[...]).astype(jnp.bfloat16)

    def mix(t, k):
        line = normed[t * tile * rows : (t + 1) * tile * rows, :]
        gate = dot(line, win_ref[:, k])
        up = dot(line, win_ref[:, slice(hidden_len + k.start, hidden_len + k.stop)])
        hidden = (0.5 * gate * (1.0 + jnp.tanh(0.5 * gate)) * up).astype(jnp.bfloat16)
        return dot(hidden, wdown_ref[k, :])

    for n in range(tile):
        smooth(n)
    chunk = hidden_len // tile
    copies = []
    for t in range(len(outs) // tile):
        update = None
        for n in range(tile):
            term = mix(t, slice(n * chunk, (n + 1) * chunk))
            update = term if update is None else update + term
            if (t + 1) * tile + n < len(outs):
                smooth((t + 1) * tile + n)
        for n in range(tile):
            source, target = outs[t * tile + n]
            kept = wide[source + MARGIN, MARGIN : MARGIN + rows, :]
            done[t * tile + n] = (kept + update[n * rows : (n + 1) * rows]).astype(jnp.bfloat16)
            copies.append(
                pltpu.make_async_copy(done.at[t * tile + n], o_ref.at[target], sems.at[t * tile + n])
            )
            copies[-1].start()
    for copy in copies:
        copy.wait()


def whole(shape):
    return pl.BlockSpec(shape, lambda *_: (0,) * len(shape))


def split_weights(qkv, features):
    keys = qkv[:, features : 2 * features]
    both = jnp.concatenate([qkv[:, :features], qkv[:, 2 * features :]], 1).T
    return keys, both


SMEM = pl.BlockSpec(memory_space=pltpu.SMEM)
VMEM = pl.BlockSpec(memory_space=pltpu.VMEM)


def cost(cells, length, features, heads):
    return pl.CostEstimate(
        flops=2 * cells * features * (4 * features + (heads + 2) * length),
        bytes_accessed=4 * cells * features,
        transcendentals=cells * length * heads,
    )


def lon_call(lines, factors, gains, qkv, out_w, bands, blocks, count, sizes):
    all_cols, rows, features = lines.shape
    heads = factors.shape[0]
    wk, wqv = split_weights(qkv, features)
    unroll = next(u for u in (8, 2, 1) if u == 1 or (count % u == 0 and all_cols <= 2 * LANES))
    return pl.pallas_call(
        functools.partial(lon_kernel, bands=bands, blocks=blocks, count=count),
        out_shape=[
            jax.ShapeDtypeStruct((bands * blocks, size, rows, features), jnp.bfloat16) for size in sizes
        ],
        in_specs=[SMEM] + [VMEM] * 5,
        out_specs=[VMEM] * len(sizes),
        scratch_shapes=[
            pltpu.VMEM((features // LANES, all_cols * rows, LANES), jnp.float32),
            pltpu.VMEM((features // LANES, all_cols * rows, LANES), jnp.float32),
            pltpu.VMEM((heads * unroll, features, padded(all_cols, LANES)), jnp.bfloat16),
        ],
        cost_estimate=cost(all_cols * count, all_cols, features, heads),
        name="lon_attention",
    )(factors, lines, gains, wk, wqv, out_w)


def lat_call(columns, factors, gains, qkv, out_w, bands):
    sources, count, rows, features = columns.shape
    heads = factors.shape[0]
    length = sources * rows
    tall = length // bands + 2 * MARGIN
    wk, wqv = split_weights(qkv, features)
    return pl.pallas_call(
        functools.partial(lat_kernel, bands=bands),
        grid=(count,),
        out_shape=jax.ShapeDtypeStruct((bands, count, tall, features), jnp.bfloat16),
        in_specs=[
            SMEM,
            pl.BlockSpec((sources, 1, rows, features), lambda k: (0, k, 0, 0)),
            whole((1, features)),
            whole((features, features)),
            whole((2 * features, features)),
            whole((features, features)),
        ],
        out_specs=pl.BlockSpec((bands, 1, tall, features), lambda k: (0, k, 0, 0)),
        scratch_shapes=[
            pltpu.VMEM((length + 16, features), jnp.float32),
            pltpu.VMEM((heads, features, length), jnp.bfloat16),
        ],
        cost_estimate=cost(count * length, length, features, heads),
        name="lat_attention",
    )(factors, columns, gains, wk, wqv, out_w)


def mixer_call(inputs, strips, cols, out, taps, gains, win, wdown):
    _, tall, features = inputs[0].shape
    rows = tall - 2 * MARGIN
    held = sum(high - low for _, pieces in strips for _, low, high in pieces)
    count = held - 2 * MARGIN * len(strips)
    tile = next(n for n in (4, 2, 1) if count % n == 0)
    some = pl.BlockSpec(memory_space=pl.ANY)
    before = [] if out is None else [out]
    return pl.pallas_call(
        functools.partial(mixer_kernel, strips=strips, filled=len(before), tile=tile),
        out_shape=jax.ShapeDtypeStruct((cols, rows, features), jnp.bfloat16),
        in_specs=[VMEM] * (len(inputs) + 4) + [some] * len(before),
        out_specs=some,
        scratch_shapes=[
            pltpu.VMEM((held, padded(tall, 8), features), jnp.float32),
            pltpu.VMEM((count * rows, features), jnp.bfloat16),
            pltpu.VMEM((count, rows, features), jnp.bfloat16),
            pltpu.SemaphoreType.DMA((count,)),
        ],
        input_output_aliases={len(inputs) + 4: 0} if before else {},
        cost_estimate=pl.CostEstimate(
            flops=2 * count * rows * features * 3 * wdown.shape[0],
            bytes_accessed=4 * count * rows * features,
            transcendentals=count * rows * wdown.shape[0],
        ),
        name="mixer",
    )(*inputs, taps, gains, win, wdown, *before)


def per_device(
    fields,
    norm_gains,
    lon_qkv,
    lon_out,
    lat_qkv,
    lat_out,
    logit_scales,
    conv_taps,
    mlp_in,
    mlp_down,
):
    lat_rows, lon_cols, features = fields.shape
    blocks = lax.axis_size("lon")
    bands = lax.axis_size("lat")
    sub_rows = lat_rows // blocks
    tall_rows = padded(sub_rows, 8)
    sub_cols = lon_cols // bands
    all_cols = lon_cols * blocks
    all_rows = lat_rows * bands
    tall = lat_rows + 2 * MARGIN
    factors = logit_scales * LOG2E

    stacked = jnp.transpose(fields.reshape(blocks, sub_rows, lon_cols, features), (0, 2, 1, 3))
    if tall_rows > sub_rows:
        stacked = jnp.pad(stacked, ((0, 0), (0, 0), (0, tall_rows - sub_rows), (0, 0)))
    lines = lax.all_to_all(stacked, "lon", split_axis=0, concat_axis=0, tiled=True)
    lines = lines.reshape(all_cols, tall_rows, features)
    sizes = [n for n in (sub_cols - sub_cols // 2, sub_cols // 2) if n]
    first_state = lon_call(
        lines, factors[0], norm_gains[0:1], lon_qkv, lon_out, bands, blocks, sub_rows, sizes
    )

    parts = []
    for size, state in zip(sizes, first_state):
        columns = lax.all_to_all(state, ("lat", "lon"), split_axis=0, concat_axis=0, tiled=True)
        if tall_rows > sub_rows:
            columns = jnp.swapaxes(columns[:, :, :sub_rows], 0, 1).reshape(1, size, all_rows, features)
        second = lat_call(columns, factors[1], norm_gains[1:2], lat_qkv, lat_out, bands)
        block = lax.all_to_all(second, "lat", split_axis=0, concat_axis=0, tiled=True)
        parts.append(block.reshape(bands * size, tall, features))

    left, right = parts
    shared, rest = left.shape[0], right.shape[0]
    up = [(i, (i + 1) % blocks) for i in range(blocks)]
    after = lax.ppermute(left[:MARGIN], "lon", [(j, i) for i, j in up])
    before = lax.ppermute(right[rest - MARGIN :], "lon", up)
    mixer = (conv_taps, norm_gains[2:3], mlp_in, mlp_down)
    edge = 2 * MARGIN
    out = mixer_call([left], [(MARGIN, [(0, 0, shared)])], lon_cols, None, *mixer)
    strips = [(shared - MARGIN, [(0, shared - edge, shared), (1, 0, rest)])]
    out = mixer_call([left, right], strips, lon_cols, out, *mixer)
    strips = [
        (0, [(2, 0, MARGIN), (0, 0, edge)]),
        (lon_cols - MARGIN, [(1, rest - edge, rest), (3, 0, MARGIN)]),
    ]
    out = mixer_call([left, right, before, after], strips, lon_cols, out, *mixer)
    return jnp.transpose(out, (1, 0, 2))


def solution(mesh):
    in_specs = (P(("groups", "lat"), "lon", None), P(), P(), P(), P(), P(), P(), P(), P(), P())
    out_specs = P(("groups", "lat"), "lon", None)
    return jax.shard_map(
        per_device, mesh=mesh, in_specs=in_specs, out_specs=out_specs, check_vma=False
    )
```

```python
import functools

import jax
import jax.numpy as jnp
from jax import lax
from jax.experimental import pallas as pl
from jax.experimental.pallas import tpu as pltpu
from jax.sharding import PartitionSpec as P

KERNEL = 5
MARGIN = KERNEL // 2
EPSILON = 1e-05
LOG2E = 1.4426950408889634
LANES = 128

NT = (((1,), (1,)), ((), ()))
TN = (((0,), (0,)), ((), ()))


def dot(a, b, dims=(((1,), (0,)), ((), ()))):
    return lax.dot_general(a, b, dims, preferred_element_type=jnp.float32)


def padded(n, unit):
    return -(-n // unit) * unit


def layer_norm(values, gains):
    average = jnp.mean(values, -1, keepdims=True)
    centred = values - average
    spread = jnp.mean(centred * centred, -1, keepdims=True)
    return centred * lax.rsqrt(spread + EPSILON) * gains


def attend_line(keys, both, factors, diag, out_w, group):
    features = keys.shape[1]
    heads = len(factors)
    size = features // heads
    parts = [None] * heads
    for h in range(heads):
        rows = slice(h * size, (h + 1) * size)
        diag[h, rows, :] = both[rows]
    for start in range(0, heads, group):
        some = range(start, start + group)
        scores = {h: dot(keys, diag[h]) for h in some}
        rounded, total = {}, {}
        for h in some:
            top = jnp.max(scores[h], 0, keepdims=True)
            weights = jnp.exp2((scores[h] - top) * factors[h])
            total[h] = jnp.sum(weights, 0, keepdims=True)
            rounded[h] = weights.astype(jnp.bfloat16)
        for h in some:
            values = both[features + h * size : features + (h + 1) * size]
            parts[h] = (dot(values, rounded[h]) / total[h]).astype(jnp.bfloat16)
    return dot(jnp.concatenate(parts, 0), out_w, TN)


def attend_lines(keys, both, factors, diag, out_w, count, width, heads, lines):
    features = keys.shape[1]
    size = features // heads
    pairs = [(u, h) for u in range(lines) for h in range(heads)]
    parts = {}
    scores = {}
    for u, h in pairs:
        rows = slice(h * size, (h + 1) * size)
        diag[u * heads + h, rows, :] = both[rows, u * width : (u + 1) * width]
    for u, h in pairs:
        scores[u, h] = dot(keys[u * width : u * width + count], diag[u * heads + h])
    rounded, total = {}, {}
    for u, h in pairs:
        top = jnp.max(scores[u, h], 0, keepdims=True)
        weights = jnp.exp2((scores[u, h] - top) * factors[h])
        total[u, h] = jnp.sum(weights, 0, keepdims=True)
        packed = weights.astype(jnp.bfloat16)
        if width > count:
            packed = jnp.concatenate([packed, jnp.zeros((width - count, width), jnp.bfloat16)], 0)
        rounded[u, h] = packed
    for u, h in pairs:
        values = both[features + h * size : features + (h + 1) * size, u * width : (u + 1) * width]
        parts[u, h] = (dot(values, rounded[u, h]) / total[u, h]).astype(jnp.bfloat16)
    context = [jnp.concatenate([parts[u, h] for h in range(heads)], 0) for u in range(lines)]
    return dot(jnp.concatenate(context, 1), out_w, TN)


def lon_kernel(factor_ref, x_ref, gain_ref, wk_ref, wqv_ref, wo_ref, *rest, bands, blocks, count):
    *o_refs, state, normed, diag = rest
    cols, rows, features = x_ref.shape
    heads = factor_ref.shape[0]
    width = diag.shape[2]
    diag[...] = jnp.zeros_like(diag)
    step = cols // bands
    lanes = [slice(c, c + LANES) for c in range(0, features, LANES)]

    @pl.loop(0, bands)
    def _(i):
        x = x_ref[pl.ds(i * step, step)].astype(jnp.float32).reshape(step * rows, features)
        y = layer_norm(x, gain_ref[...])
        at = pl.ds(pl.multiple_of(i * step * rows, 8), step * rows)
        for c, part in enumerate(lanes):
            state[c, at, :] = x[:, part]
            normed[c, at, :] = y[:, part]

    factors = [factor_ref[h] for h in range(heads)]

    unroll = diag.shape[0] // heads

    @pl.loop(0, count // unroll)
    def _(group):
        spots = [pl.ds(group * unroll + u, cols, stride=rows) for u in range(unroll)]
        lines = []
        for at in spots:
            line = [normed.at[c][at, :].astype(jnp.bfloat16) for c in range(len(lanes))]
            line = jnp.concatenate(line, 1)
            if width > cols:
                line = jnp.concatenate([line, jnp.zeros((width - cols, features), jnp.bfloat16)], 0)
            lines.append(line)
        stack = jnp.concatenate(lines, 0)
        keys = dot(stack, wk_ref[...]).astype(jnp.bfloat16)
        both = dot(wqv_ref[...], stack, NT).astype(jnp.bfloat16)
        mixes = attend_lines(keys, both, factors, diag, wo_ref[...], cols, width, heads, unroll)
        for u, at in enumerate(spots):
            mix = mixes[u * width : u * width + cols].astype(jnp.bfloat16).astype(jnp.float32)
            for c, part in enumerate(lanes):
                state.at[c][at, :] = state.at[c][at, :] + mix[:, part]

    first = 0
    for o_ref in o_refs:
        size = o_ref.shape[1]
        for i in range(bands):
            for j in range(blocks):
                start = (j * (cols // blocks) + first + i * size) * rows
                at = slice(start, start + size * rows)
                y = jnp.concatenate([state[c, at, :] for c in range(len(lanes))], 1)
                o_ref[i * blocks + j] = y.reshape(size, rows, features).astype(jnp.bfloat16)
        first += bands * size


def lat_kernel(factor_ref, x_ref, gain_ref, wk_ref, wqv_ref, wo_ref, o_ref, state, diag, *, bands):
    sources, _, rows, features = x_ref.shape
    length = sources * rows
    heads = diag.shape[0]

    @pl.when(pl.program_id(0) == 0)
    def _():
        diag[...] = jnp.zeros_like(diag)
        state[...] = jnp.zeros_like(state)

    x = x_ref[:, 0].astype(jnp.float32).reshape(length, features)
    line = layer_norm(x, gain_ref[...]).astype(jnp.bfloat16)
    keys = dot(line, wk_ref[...]).astype(jnp.bfloat16)
    both = dot(wqv_ref[...], line, NT).astype(jnp.bfloat16)
    factors = [factor_ref[h] for h in range(heads)]
    mix = attend_line(keys, both, factors, diag, wo_ref[...], 8)
    state[8 : 8 + length, :] = x + mix.astype(jnp.bfloat16).astype(jnp.float32)
    band = length // bands
    for i in range(bands):
        first = 8 + i * band - MARGIN
        o_ref[i, 0] = state[first : first + o_ref.shape[2], :].astype(jnp.bfloat16)


def mixer_kernel(*refs, strips, filled, tile):
    count = 1 + max(piece[0] for _, pieces in strips for piece in pieces)
    inputs = refs[:count]
    taps_ref, gain_ref, win_ref, wdown_ref = refs[count : count + 4]
    o_ref, wide, normed, done, sems = refs[count + 4 + filled :]
    tall, features = inputs[0].shape[1:]
    rows = o_ref.shape[1]
    hidden_len = wdown_ref.shape[0]
    outs, at = [], 0
    for first, pieces in strips:
        start = at
        for index, low, high in pieces:
            wide[at : at + high - low] = inputs[index][low:high].astype(jnp.float32)
            at += high - low
        outs += [(start + c, first + c) for c in range(at - start - 2 * MARGIN)]

    def smooth(n):
        source = outs[n][0]
        total = None
        for dy in range(KERNEL):
            part = None
            for dx in range(KERNEL):
                tap = taps_ref[dy * KERNEL + dx : dy * KERNEL + dx + 1, :]
                term = wide[source + dx] * tap
                part = term if part is None else part + term
            part = part[dy : dy + rows]
            total = part if total is None else total + part
        normed[n * rows : (n + 1) * rows, :] = layer_norm(total, gain_ref[...]).astype(jnp.bfloat16)

    def mix(t, k):
        line = normed[t * tile * rows : (t + 1) * tile * rows, :]
        gate = dot(line, win_ref[:, k])
        up = dot(line, win_ref[:, slice(hidden_len + k.start, hidden_len + k.stop)])
        hidden = (0.5 * gate * (1.0 + jnp.tanh(0.5 * gate)) * up).astype(jnp.bfloat16)
        return dot(hidden, wdown_ref[k, :])

    for n in range(tile):
        smooth(n)
    chunk = hidden_len // tile
    copies = []
    for t in range(len(outs) // tile):
        update = None
        for n in range(tile):
            term = mix(t, slice(n * chunk, (n + 1) * chunk))
            update = term if update is None else update + term
            if (t + 1) * tile + n < len(outs):
                smooth((t + 1) * tile + n)
        for n in range(tile):
            source, target = outs[t * tile + n]
            kept = wide[source + MARGIN, MARGIN : MARGIN + rows, :]
            done[t * tile + n] = (kept + update[n * rows : (n + 1) * rows]).astype(jnp.bfloat16)
            copies.append(
                pltpu.make_async_copy(done.at[t * tile + n], o_ref.at[target], sems.at[t * tile + n])
            )
            copies[-1].start()
    for copy in copies:
        copy.wait()


def whole(shape):
    return pl.BlockSpec(shape, lambda *_: (0,) * len(shape))


def split_weights(qkv, features):
    keys = qkv[:, features : 2 * features]
    both = jnp.concatenate([qkv[:, :features], qkv[:, 2 * features :]], 1).T
    return keys, both


SMEM = pl.BlockSpec(memory_space=pltpu.SMEM)
VMEM = pl.BlockSpec(memory_space=pltpu.VMEM)


def cost(cells, length, features, heads):
    return pl.CostEstimate(
        flops=2 * cells * features * (4 * features + (heads + 2) * length),
        bytes_accessed=4 * cells * features,
        transcendentals=cells * length * heads,
    )


def lon_call(lines, factors, gains, qkv, out_w, bands, blocks, count, sizes):
    all_cols, rows, features = lines.shape
    heads = factors.shape[0]
    wk, wqv = split_weights(qkv, features)
    unroll = next(u for u in (8, 2, 1) if u == 1 or (count % u == 0 and all_cols <= 2 * LANES))
    return pl.pallas_call(
        functools.partial(lon_kernel, bands=bands, blocks=blocks, count=count),
        out_shape=[
            jax.ShapeDtypeStruct((bands * blocks, size, rows, features), jnp.bfloat16) for size in sizes
        ],
        in_specs=[SMEM] + [VMEM] * 5,
        out_specs=[VMEM] * len(sizes),
        scratch_shapes=[
            pltpu.VMEM((features // LANES, all_cols * rows, LANES), jnp.float32),
            pltpu.VMEM((features // LANES, all_cols * rows, LANES), jnp.float32),
            pltpu.VMEM((heads * unroll, features, padded(all_cols, LANES)), jnp.bfloat16),
        ],
        cost_estimate=cost(all_cols * count, all_cols, features, heads),
        name="lon_attention",
    )(factors, lines, gains, wk, wqv, out_w)


def lat_call(columns, factors, gains, qkv, out_w, bands):
    sources, count, rows, features = columns.shape
    heads = factors.shape[0]
    length = sources * rows
    tall = padded(length // bands + 2 * MARGIN, 8)
    wk, wqv = split_weights(qkv, features)
    return pl.pallas_call(
        functools.partial(lat_kernel, bands=bands),
        grid=(count,),
        out_shape=jax.ShapeDtypeStruct((bands, count, tall, features), jnp.bfloat16),
        in_specs=[
            SMEM,
            pl.BlockSpec((sources, 1, rows, features), lambda k: (0, k, 0, 0)),
            whole((1, features)),
            whole((features, features)),
            whole((2 * features, features)),
            whole((features, features)),
        ],
        out_specs=pl.BlockSpec((bands, 1, tall, features), lambda k: (0, k, 0, 0)),
        scratch_shapes=[
            pltpu.VMEM((length + 8 + tall - length // bands, features), jnp.float32),
            pltpu.VMEM((heads, features, length), jnp.bfloat16),
        ],
        cost_estimate=cost(count * length, length, features, heads),
        name="lat_attention",
    )(factors, columns, gains, wk, wqv, out_w)


def mixer_call(inputs, strips, cols, rows, out, taps, gains, win, wdown):
    _, tall, features = inputs[0].shape
    held = sum(high - low for _, pieces in strips for _, low, high in pieces)
    count = held - 2 * MARGIN * len(strips)
    tile = next(n for n in (4, 2, 1) if count % n == 0)
    some = pl.BlockSpec(memory_space=pl.ANY)
    before = [] if out is None else [out]
    return pl.pallas_call(
        functools.partial(mixer_kernel, strips=strips, filled=len(before), tile=tile),
        out_shape=jax.ShapeDtypeStruct((cols, rows, features), jnp.bfloat16),
        in_specs=[VMEM] * (len(inputs) + 4) + [some] * len(before),
        out_specs=some,
        scratch_shapes=[
            pltpu.VMEM((held, tall, features), jnp.float32),
            pltpu.VMEM((count * rows, features), jnp.bfloat16),
            pltpu.VMEM((count, rows, features), jnp.bfloat16),
            pltpu.SemaphoreType.DMA((count,)),
        ],
        input_output_aliases={len(inputs) + 4: 0} if before else {},
        cost_estimate=pl.CostEstimate(
            flops=2 * count * rows * features * 3 * wdown.shape[0],
            bytes_accessed=4 * count * rows * features,
            transcendentals=count * rows * wdown.shape[0],
        ),
        name="mixer",
    )(*inputs, taps, gains, win, wdown, *before)


def per_device(
    fields,
    norm_gains,
    lon_qkv,
    lon_out,
    lat_qkv,
    lat_out,
    logit_scales,
    conv_taps,
    mlp_in,
    mlp_down,
):
    lat_rows, lon_cols, features = fields.shape
    blocks = lax.axis_size("lon")
    bands = lax.axis_size("lat")
    sub_rows = lat_rows // blocks
    tall_rows = padded(sub_rows, 8)
    sub_cols = lon_cols // bands
    all_cols = lon_cols * blocks
    all_rows = lat_rows * bands
    tall = padded(lat_rows + 2 * MARGIN, 8)
    factors = logit_scales * LOG2E

    stacked = jnp.transpose(fields.reshape(blocks, sub_rows, lon_cols, features), (0, 2, 1, 3))
    if tall_rows > sub_rows:
        stacked = jnp.pad(stacked, ((0, 0), (0, 0), (0, tall_rows - sub_rows), (0, 0)))
    lines = lax.all_to_all(stacked, "lon", split_axis=0, concat_axis=0, tiled=True)
    lines = lines.reshape(all_cols, tall_rows, features)
    sizes = [n for n in (sub_cols - sub_cols // 2, sub_cols // 2) if n]
    first_state = lon_call(
        lines, factors[0], norm_gains[0:1], lon_qkv, lon_out, bands, blocks, sub_rows, sizes
    )

    def to_columns(state):
        columns = lax.all_to_all(state, ("lat", "lon"), split_axis=0, concat_axis=0, tiled=True)
        if tall_rows > sub_rows:
            columns = jnp.swapaxes(columns[:, :, :sub_rows], 0, 1)
            columns = columns.reshape(1, columns.shape[0], all_rows, features)
        return columns

    def to_block(state):
        block = lax.all_to_all(state, "lat", split_axis=0, concat_axis=0, tiled=True)
        return block.reshape(-1, tall, features)

    def attend(columns):
        return lat_call(columns, factors[1], norm_gains[1:2], lat_qkv, lat_out, bands)

    near, far = first_state
    near = to_columns(near)
    near, far = lax.optimization_barrier((near, far))
    far = to_columns(far)
    near = attend(near)
    near, far = lax.optimization_barrier((near, far))
    left = to_block(near)
    far = attend(far)
    left, far = lax.optimization_barrier((left, far))
    right = to_block(far)

    shared, rest = left.shape[0], right.shape[0]
    up = [(i, (i + 1) % blocks) for i in range(blocks)]
    after = lax.ppermute(left[:MARGIN], "lon", [(j, i) for i, j in up])
    before = lax.ppermute(right[rest - MARGIN :], "lon", up)
    mixer = (conv_taps, norm_gains[2:3], mlp_in, mlp_down)
    edge = 2 * MARGIN
    out = mixer_call([left], [(MARGIN, [(0, 0, shared)])], lon_cols, lat_rows, None, *mixer)
    strips = [(shared - MARGIN, [(0, shared - edge, shared), (1, 0, rest)])]
    out = mixer_call([left, right], strips, lon_cols, lat_rows, out, *mixer)
    strips = [
        (0, [(2, 0, MARGIN), (0, 0, edge)]),
        (lon_cols - MARGIN, [(1, rest - edge, rest), (3, 0, MARGIN)]),
    ]
    out = mixer_call([left, right, before, after], strips, lon_cols, lat_rows, out, *mixer)
    return jnp.transpose(out, (1, 0, 2))


def solution(mesh):
    in_specs = (P(("groups", "lat"), "lon", None), P(), P(), P(), P(), P(), P(), P(), P(), P())
    out_specs = P(("groups", "lat"), "lon", None)
    return jax.shard_map(
        per_device, mesh=mesh, in_specs=in_specs, out_specs=out_specs, check_vma=False
    )
```

```python
import functools

import jax
import jax.numpy as jnp
from jax import lax
from jax.experimental import pallas as pl
from jax.experimental.pallas import tpu as pltpu
from jax.sharding import PartitionSpec as P

KERNEL = 5
MARGIN = KERNEL // 2
EPSILON = 1e-05
LOG2E = 1.4426950408889634
LANES = 128

NT = (((1,), (1,)), ((), ()))
TN = (((0,), (0,)), ((), ()))


def dot(a, b, dims=(((1,), (0,)), ((), ()))):
    return lax.dot_general(a, b, dims, preferred_element_type=jnp.float32)


def padded(n, unit):
    return -(-n // unit) * unit


def layer_norm(values, gains):
    average = jnp.mean(values, -1, keepdims=True)
    centred = values - average
    spread = jnp.mean(centred * centred, -1, keepdims=True)
    return centred * lax.rsqrt(spread + EPSILON) * gains


def attend_line(keys, both, factors, diag, out_w):
    length, features = keys.shape
    heads = len(factors)
    size = features // heads
    joined = diag.shape[2] // length
    for h in range(heads):
        rows = slice(h * size, (h + 1) * size)
        lane = h % joined * length
        diag[h // joined, rows, lane : lane + length] = both[rows]
    groups = heads // joined
    scores, rounded, total, parts = {}, {}, {}, []

    def soften(h):
        lane = h % joined * length
        score = scores[h // joined][:, lane : lane + length]
        top = jnp.max(score, 0, keepdims=True)
        weights = jnp.exp2((score - top) * factors[h])
        total[h] = jnp.sum(weights, 0, keepdims=True)
        rounded[h] = weights.astype(jnp.bfloat16)

    def gather(h):
        values = both[features + h * size : features + (h + 1) * size]
        parts.append((dot(values, rounded[h]) / total[h]).astype(jnp.bfloat16))

    for p in range(groups + 1 + 1):
        if p < groups:
            scores[p] = dot(keys, diag[p])
        if 0 <= p - 1 < groups:
            for h in range((p - 1) * joined, (p - 1 + 1) * joined):
                soften(h)
        if 0 <= p - 1 - 1 < groups:
            for h in range((p - 1 - 1) * joined, (p - 1 - 1 + 1) * joined):
                gather(h)
    return dot(jnp.concatenate(parts, 0), out_w, TN)


def attend_lines(keys, both, factors, diag, out_w, count, width, lines):
    features = keys.shape[1]
    heads = len(factors)
    size = features // heads
    joined = diag.shape[2] // width
    groups = heads // joined
    for u in range(lines):
        for h in range(heads):
            rows = slice(h * size, (h + 1) * size)
            lane = h % joined * width
            diag[u * groups + h // joined, rows, lane : lane + width] = both[rows, u * width : (u + 1) * width]
    scores = [
        [dot(keys[u * width : u * width + count], diag[u * groups + p]) for p in range(groups)]
        for u in range(lines)
    ]
    pairs = [(u, h) for u in range(lines) for h in range(heads)]
    rounded, total = {}, {}
    for u, h in pairs:
        lane = h % joined * width
        score = scores[u][h // joined][:, lane : lane + width]
        top = jnp.max(score, 0, keepdims=True)
        weights = jnp.exp2((score - top) * factors[h])
        total[u, h] = jnp.sum(weights, 0, keepdims=True)
        packed = weights.astype(jnp.bfloat16)
        if width > count:
            packed = jnp.concatenate([packed, jnp.zeros((width - count, width), jnp.bfloat16)], 0)
        rounded[u, h] = packed
    parts = {}
    for u, h in pairs:
        values = both[features + h * size : features + (h + 1) * size, u * width : (u + 1) * width]
        parts[u, h] = (dot(values, rounded[u, h]) / total[u, h]).astype(jnp.bfloat16)
    context = [jnp.concatenate([parts[u, h] for h in range(heads)], 0) for u in range(lines)]
    return dot(jnp.concatenate(context, 1), out_w, TN)


def lon_kernel(factor_ref, place_ref, *refs, blocks, bands, count, filled):
    pieces = refs[:blocks]
    gain_ref, wk_ref, wqv_ref, wo_ref = refs[blocks : blocks + 4]
    *o_refs, state, normed, diag = refs[blocks + 4 + filled :]
    part_cols, rows, features = pieces[0].shape
    cols = blocks * part_cols
    heads = factor_ref.shape[0]
    width = padded(cols, LANES)
    diag[...] = jnp.zeros_like(diag)
    lanes = [slice(c, c + LANES) for c in range(0, features, LANES)]
    for k, piece in enumerate(pieces):
        source = lax.rem(place_ref[0] + (blocks - k), blocks)
        x = piece[...].astype(jnp.float32).reshape(part_cols * rows, features)
        y = layer_norm(x, gain_ref[...])
        at = pl.ds(pl.multiple_of(source * (part_cols * rows), 8), part_cols * rows)
        for c, part in enumerate(lanes):
            state[c, at, :] = x[:, part]
            normed[c, at, :] = y[:, part]

    factors = [factor_ref[h] for h in range(heads)]

    unroll = diag.shape[0] * diag.shape[2] // (heads * width)

    @pl.loop(0, count // unroll)
    def _(group):
        spots = [pl.ds(group * unroll + u, cols, stride=rows) for u in range(unroll)]
        lines = []
        for at in spots:
            line = [normed.at[c][at, :].astype(jnp.bfloat16) for c in range(len(lanes))]
            line = jnp.concatenate(line, 1)
            if width > cols:
                line = jnp.concatenate([line, jnp.zeros((width - cols, features), jnp.bfloat16)], 0)
            lines.append(line)
        stack = jnp.concatenate(lines, 0)
        keys = dot(stack, wk_ref[...]).astype(jnp.bfloat16)
        both = dot(wqv_ref[...], stack, NT).astype(jnp.bfloat16)
        mixes = attend_lines(keys, both, factors, diag, wo_ref[...], cols, width, unroll)
        for u, at in enumerate(spots):
            mix = mixes[u * width : u * width + cols].astype(jnp.bfloat16).astype(jnp.float32)
            for c, part in enumerate(lanes):
                state.at[c][at, :] = state.at[c][at, :] + mix[:, part]

    first = 0
    for o_ref in o_refs:
        size = o_ref.shape[1]
        for i in range(bands):
            for j in range(blocks):
                start = (j * (cols // blocks) + first + i * size) * rows
                at = slice(start, start + size * rows)
                y = jnp.concatenate([state[c, at, :] for c in range(len(lanes))], 1)
                o_ref[i * blocks + j] = y.reshape(size, rows, features).astype(jnp.bfloat16)
        first += bands * size


def lat_kernel(factor_ref, x_ref, gain_ref, wk_ref, wqv_ref, wo_ref, o_ref, state, diag, *, bands):
    sources, _, rows, features = x_ref.shape
    length = sources * rows
    heads = factor_ref.shape[0]

    @pl.when(pl.program_id(0) == 0)
    def _():
        diag[...] = jnp.zeros_like(diag)
        state[...] = jnp.zeros_like(state)

    x = x_ref[:, 0].astype(jnp.float32).reshape(length, features)
    line = layer_norm(x, gain_ref[...]).astype(jnp.bfloat16)
    keys = dot(line, wk_ref[...]).astype(jnp.bfloat16)
    both = dot(wqv_ref[...], line, NT).astype(jnp.bfloat16)
    factors = [factor_ref[h] for h in range(heads)]
    mix = attend_line(keys, both, factors, diag, wo_ref[...])
    state[8 : 8 + length, :] = x + mix.astype(jnp.bfloat16).astype(jnp.float32)
    band = length // bands
    for i in range(bands):
        first = 8 + i * band - MARGIN
        o_ref[i, 0] = state[first : first + o_ref.shape[2], :].astype(jnp.bfloat16)


def mixer_kernel(*refs, strips, filled, tile):
    count = 1 + max(piece[0] for _, pieces in strips for piece in pieces)
    inputs = refs[:count]
    taps_ref, gain_ref, win_ref, wdown_ref = refs[count : count + 4]
    o_ref, wide, normed, done, sems = refs[count + 4 + filled :]
    tall, features = inputs[0].shape[1:]
    rows = o_ref.shape[1]
    hidden_len = wdown_ref.shape[0]
    outs, at = [], 0
    for first, pieces in strips:
        start = at
        for index, low, high in pieces:
            wide[at : at + high - low] = inputs[index][low:high].astype(jnp.float32)
            at += high - low
        outs += [(start + c, first + c) for c in range(at - start - 2 * MARGIN)]

    def smooth(n):
        source = outs[n][0]
        total = None
        for dy in range(KERNEL):
            part = None
            for dx in range(KERNEL):
                tap = taps_ref[dy * KERNEL + dx : dy * KERNEL + dx + 1, :]
                term = wide[source + dx] * tap
                part = term if part is None else part + term
            part = part[dy : dy + rows]
            total = part if total is None else total + part
        normed[n * rows : (n + 1) * rows, :] = layer_norm(total, gain_ref[...]).astype(jnp.bfloat16)

    def mix(t, k):
        line = normed[t * tile * rows : (t + 1) * tile * rows, :]
        gate = dot(line, win_ref[:, k])
        up = dot(line, win_ref[:, slice(hidden_len + k.start, hidden_len + k.stop)])
        hidden = (0.5 * gate * (1.0 + jnp.tanh(0.5 * gate)) * up).astype(jnp.bfloat16)
        return dot(hidden, wdown_ref[k, :])

    for n in range(tile):
        smooth(n)
    chunk = hidden_len // tile
    copies = []
    for t in range(len(outs) // tile):
        update = None
        for n in range(tile):
            term = mix(t, slice(n * chunk, (n + 1) * chunk))
            update = term if update is None else update + term
            if (t + 1) * tile + n < len(outs):
                smooth((t + 1) * tile + n)
        for n in range(tile):
            source, target = outs[t * tile + n]
            kept = wide[source + MARGIN, MARGIN : MARGIN + rows, :]
            done[t * tile + n] = (kept + update[n * rows : (n + 1) * rows]).astype(jnp.bfloat16)
            copies.append(
                pltpu.make_async_copy(done.at[t * tile + n], o_ref.at[target], sems.at[t * tile + n])
            )
            copies[-1].start()
    for copy in copies:
        copy.wait()


def whole(shape):
    return pl.BlockSpec(shape, lambda *_: (0,) * len(shape))


def split_weights(qkv, features):
    keys = qkv[:, features : 2 * features]
    both = jnp.concatenate([qkv[:, :features], qkv[:, 2 * features :]], 1).T
    return keys, both


SMEM = pl.BlockSpec(memory_space=pltpu.SMEM)
VMEM = pl.BlockSpec(memory_space=pltpu.VMEM)


def cost(cells, length, features, heads):
    return pl.CostEstimate(
        flops=2 * cells * features * (4 * features + (heads + 2) * length),
        bytes_accessed=4 * cells * features,
        transcendentals=cells * length * heads,
    )


def params(*sizes):
    return pltpu.CompilerParams(vmem_limit_bytes=min(60 * 2**20, 2 * sum(sizes) + 2**22))


def lon_call(pieces, place, out, factors, gains, weights, out_w, bands, count, chunk, chunks, sizes):
    blocks = len(pieces)
    part_cols, rows, features = pieces[0].shape
    all_cols = blocks * part_cols
    heads = factors.shape[0]
    unroll = next(u for u in (8, 2, 1) if u == 1 or (count % u == 0 and all_cols <= 2 * LANES))
    some = pl.BlockSpec(memory_space=pl.ANY)
    return pl.pallas_call(
        functools.partial(lon_kernel, blocks=blocks, bands=bands, count=count, filled=len(out)),
        grid=(1,),
        out_shape=[
            jax.ShapeDtypeStruct((bands * blocks, size, chunks * rows, features), jnp.bfloat16)
            for size in sizes
        ],
        in_specs=[SMEM] * 2 + [VMEM] * (blocks + 4) + [some] * len(out),
        out_specs=[
            pl.BlockSpec((bands * blocks, size, rows, features), lambda _: (0, 0, chunk, 0))
            for size in sizes
        ],
        scratch_shapes=[
            pltpu.VMEM((features // LANES, all_cols * rows, LANES), jnp.float32),
            pltpu.VMEM((features // LANES, all_cols * rows, LANES), jnp.float32),
            pltpu.VMEM((heads * unroll // 2, features, 2 * padded(all_cols, LANES)), jnp.bfloat16),
        ],
        input_output_aliases={blocks + 6 + n: n for n in range(len(out))},
        cost_estimate=cost(all_cols * count, all_cols, features, heads),
        compiler_params=params(
            8 * all_cols * rows * features,
            2 * heads * unroll * features * padded(all_cols, LANES),
            4 * heads * unroll * all_cols * padded(all_cols, LANES),
        ),
        name="lon_attention",
    )(factors, place, *pieces, gains, *weights, out_w, *out)


def lat_call(columns, factors, gains, qkv, out_w, bands):
    sources, count, rows, features = columns.shape
    heads = factors.shape[0]
    length = sources * rows
    tall = padded(length // bands + 2 * MARGIN, 8)
    wk, wqv = split_weights(qkv, features)
    return pl.pallas_call(
        functools.partial(lat_kernel, bands=bands),
        grid=(count,),
        out_shape=jax.ShapeDtypeStruct((bands, count, tall, features), jnp.bfloat16),
        in_specs=[
            SMEM,
            pl.BlockSpec((sources, 1, rows, features), lambda k: (0, k, 0, 0)),
            whole((1, features)),
            whole((features, features)),
            whole((2 * features, features)),
            whole((features, features)),
        ],
        out_specs=pl.BlockSpec((bands, 1, tall, features), lambda k: (0, k, 0, 0)),
        scratch_shapes=[
            pltpu.VMEM((length + 8 + tall - length // bands, features), jnp.float32),
            pltpu.VMEM((heads // 2, features, 2 * length), jnp.bfloat16),
        ],
        cost_estimate=cost(count * length, length, features, heads),
        compiler_params=params(
            8 * length * features, 2 * heads * features * length, 4 * heads * length * length
        ),
        name="lat_attention",
    )(factors, columns, gains, wk, wqv, out_w)


def mixer_call(inputs, strips, cols, rows, out, taps, gains, win, wdown):
    _, tall, features = inputs[0].shape
    held = sum(high - low for _, pieces in strips for _, low, high in pieces)
    count = held - 2 * MARGIN * len(strips)
    tile = next(n for n in (4, 2, 1) if count % n == 0)
    some = pl.BlockSpec(memory_space=pl.ANY)
    before = [] if out is None else [out]
    return pl.pallas_call(
        functools.partial(mixer_kernel, strips=strips, filled=len(before), tile=tile),
        out_shape=jax.ShapeDtypeStruct((cols, rows, features), jnp.bfloat16),
        in_specs=[VMEM] * (len(inputs) + 4) + [some] * len(before),
        out_specs=some,
        scratch_shapes=[
            pltpu.VMEM((held, tall, features), jnp.float32),
            pltpu.VMEM((count * rows, features), jnp.bfloat16),
            pltpu.VMEM((count, rows, features), jnp.bfloat16),
            pltpu.SemaphoreType.DMA((count,)),
        ],
        input_output_aliases={len(inputs) + 4: 0} if before else {},
        cost_estimate=pl.CostEstimate(
            flops=2 * count * rows * features * 3 * wdown.shape[0],
            bytes_accessed=4 * count * rows * features,
            transcendentals=count * rows * wdown.shape[0],
        ),
        name="mixer",
    )(*inputs, taps, gains, win, wdown, *before)


def per_device(
    fields,
    norm_gains,
    lon_qkv,
    lon_out,
    lat_qkv,
    lat_out,
    logit_scales,
    conv_taps,
    mlp_in,
    mlp_down,
):
    lat_rows, lon_cols, features = fields.shape
    blocks = lax.axis_size("lon")
    bands = lax.axis_size("lat")
    sub_rows = lat_rows // blocks
    tall_rows = padded(sub_rows, 8)
    sub_cols = lon_cols // bands
    all_rows = lat_rows * bands
    tall = padded(lat_rows + 2 * MARGIN, 8)
    factors = logit_scales * LOG2E

    grid = jnp.transpose(fields, (1, 0, 2)).reshape(lon_cols, blocks, sub_rows, features)
    if tall_rows > sub_rows:
        grid = jnp.pad(grid, ((0, 0), (0, 0), (0, tall_rows - sub_rows), (0, 0)))
    grid = grid.reshape(lon_cols, blocks * tall_rows, features)
    place = lax.axis_index("lon")
    chunks = tall_rows // 8
    sizes = [sub_cols - sub_cols // 2, sub_cols // 2]
    weights = split_weights(lon_qkv, features)
    moved = []
    for chunk in range(chunks):
        pieces = []
        for k in range(blocks):
            target = lax.rem(place + k, blocks)
            piece = lax.dynamic_slice_in_dim(grid, target * tall_rows + chunk * 8, 8, 1)
            if k:
                piece = lax.ppermute(piece, "lon", [(i, (i + k) % blocks) for i in range(blocks)])
            pieces.append(piece)
        moved.append(pieces)
    first_state = []
    for chunk, pieces in enumerate(moved):
        count = min(8, sub_rows - chunk * 8)
        first_state = lon_call(
            pieces,
            place.astype(jnp.int32).reshape(1),
            first_state,
            factors[0],
            norm_gains[0:1],
            weights,
            lon_out,
            bands,
            count,
            chunk,
            chunks,
            sizes,
        )

    def to_columns(state):
        columns = lax.all_to_all(state, ("lat", "lon"), split_axis=0, concat_axis=0, tiled=True)
        if tall_rows > sub_rows:
            columns = jnp.swapaxes(columns[:, :, :sub_rows], 0, 1)
            columns = columns.reshape(1, columns.shape[0], all_rows, features)
        return columns

    def to_block(state):
        block = lax.all_to_all(state, "lat", split_axis=0, concat_axis=0, tiled=True)
        return block.reshape(-1, tall, features)

    def attend(columns):
        return lat_call(columns, factors[1], norm_gains[1:2], lat_qkv, lat_out, bands)

    near, far = first_state
    near = to_columns(near)
    near, far = lax.optimization_barrier((near, far))
    far = to_columns(far)
    near = attend(near)
    near, far = lax.optimization_barrier((near, far))
    left = to_block(near)
    far = attend(far)
    left, far = lax.optimization_barrier((left, far))
    right = to_block(far)

    shared, rest = left.shape[0], right.shape[0]
    up = [(i, (i + 1) % blocks) for i in range(blocks)]
    after = lax.ppermute(left[:MARGIN], "lon", [(j, i) for i, j in up])
    before = lax.ppermute(right[rest - MARGIN :], "lon", up)
    mixer = (conv_taps, norm_gains[2:3], mlp_in, mlp_down)
    edge = 2 * MARGIN
    out = mixer_call([left], [(MARGIN, [(0, 0, shared)])], lon_cols, lat_rows, None, *mixer)
    strips = [(shared - MARGIN, [(0, shared - edge, shared), (1, 0, rest)])]
    out = mixer_call([left, right], strips, lon_cols, lat_rows, out, *mixer)
    strips = [
        (0, [(2, 0, MARGIN), (0, 0, edge)]),
        (lon_cols - MARGIN, [(1, rest - edge, rest), (3, 0, MARGIN)]),
    ]
    out = mixer_call([left, right, before, after], strips, lon_cols, lat_rows, out, *mixer)
    return jnp.transpose(out, (1, 0, 2))


def solution(mesh):
    in_specs = (P(("groups", "lat"), "lon", None), P(), P(), P(), P(), P(), P(), P(), P(), P())
    out_specs = P(("groups", "lat"), "lon", None)
    return jax.shard_map(
        per_device, mesh=mesh, in_specs=in_specs, out_specs=out_specs, check_vma=False
    )
```

```python
import functools

import jax
import jax.numpy as jnp
from jax import lax
from jax.experimental import pallas as pl
from jax.experimental.pallas import tpu as pltpu
from jax.sharding import PartitionSpec as P

KERNEL = 5
MARGIN = KERNEL // 2
EPSILON = 1e-05
LOG2E = 1.4426950408889634
LANES = 128

NT = (((1,), (1,)), ((), ()))
TN = (((0,), (0,)), ((), ()))


def dot(a, b, dims=(((1,), (0,)), ((), ()))):
    return lax.dot_general(a, b, dims, preferred_element_type=jnp.float32)


def padded(n, unit):
    return -(-n // unit) * unit


def layer_norm(values, gains):
    average = jnp.mean(values, -1, keepdims=True)
    centred = values - average
    spread = jnp.mean(centred * centred, -1, keepdims=True)
    return centred * lax.rsqrt(spread + EPSILON) * gains


def attend_line(keys, both, factors, diag, out_w):
    length, features = keys.shape
    heads = len(factors)
    size = features // heads
    joined = diag.shape[2] // length
    for h in range(heads):
        rows = slice(h * size, (h + 1) * size)
        lane = h % joined * length
        diag[h // joined, rows, lane : lane + length] = both[rows]
    groups = heads // joined
    scores, rounded, total, parts = {}, {}, {}, []

    def soften(h):
        lane = h % joined * length
        score = scores[h // joined][:, lane : lane + length]
        top = jnp.max(score, 0, keepdims=True)
        weights = jnp.exp2((score - top) * factors[h])
        total[h] = jnp.sum(weights, 0, keepdims=True)
        rounded[h] = weights.astype(jnp.bfloat16)

    def gather(h):
        values = both[features + h * size : features + (h + 1) * size]
        parts.append((dot(values, rounded[h]) / total[h]).astype(jnp.bfloat16))

    for p in range(groups + 1 + 1):
        if p < groups:
            scores[p] = dot(keys, diag[p])
        if 0 <= p - 1 < groups:
            for h in range((p - 1) * joined, (p - 1 + 1) * joined):
                soften(h)
        if 0 <= p - 1 - 1 < groups:
            for h in range((p - 1 - 1) * joined, (p - 1 - 1 + 1) * joined):
                gather(h)
    return dot(jnp.concatenate(parts, 0), out_w, TN)


def attend_lines(keys, both, factors, diag, out_w, count, width, lines):
    features = keys.shape[1]
    heads = len(factors)
    size = features // heads
    joined = diag.shape[2] // width
    groups = heads // joined
    for u in range(lines):
        for h in range(heads):
            rows = slice(h * size, (h + 1) * size)
            lane = h % joined * width
            diag[u * groups + h // joined, rows, lane : lane + width] = both[rows, u * width : (u + 1) * width]
    scores = [
        [dot(keys[u * width : u * width + count], diag[u * groups + p]) for p in range(groups)]
        for u in range(lines)
    ]
    pairs = [(u, h) for u in range(lines) for h in range(heads)]
    rounded, total = {}, {}
    for u, h in pairs:
        lane = h % joined * width
        score = scores[u][h // joined][:, lane : lane + width]
        top = jnp.max(score, 0, keepdims=True)
        weights = jnp.exp2((score - top) * factors[h])
        total[u, h] = jnp.sum(weights, 0, keepdims=True)
        packed = weights.astype(jnp.bfloat16)
        if width > count:
            packed = jnp.concatenate([packed, jnp.zeros((width - count, width), jnp.bfloat16)], 0)
        rounded[u, h] = packed
    parts = {}
    for u, h in pairs:
        values = both[features + h * size : features + (h + 1) * size, u * width : (u + 1) * width]
        parts[u, h] = (dot(values, rounded[u, h]) / total[u, h]).astype(jnp.bfloat16)
    context = [jnp.concatenate([parts[u, h] for h in range(heads)], 0) for u in range(lines)]
    return dot(jnp.concatenate(context, 1), out_w, TN)


def lon_kernel(factor_ref, place_ref, *refs, blocks, bands, count, filled):
    pieces = refs[:blocks]
    gain_ref, wk_ref, wqv_ref, wo_ref = refs[blocks : blocks + 4]
    *o_refs, state, normed, diag = refs[blocks + 4 + filled :]
    part_cols, rows, features = pieces[0].shape
    cols = blocks * part_cols
    heads = factor_ref.shape[0]
    width = padded(cols, LANES)
    diag[...] = jnp.zeros_like(diag)
    lanes = [slice(c, c + LANES) for c in range(0, features, LANES)]
    for k, piece in enumerate(pieces):
        source = lax.rem(place_ref[0] + (blocks - k), blocks)
        x = piece[...].astype(jnp.float32).reshape(part_cols * rows, features)
        y = layer_norm(x, gain_ref[...])
        at = pl.ds(pl.multiple_of(source * (part_cols * rows), 8), part_cols * rows)
        for c, part in enumerate(lanes):
            state[c, at, :] = x[:, part]
            normed[c, at, :] = y[:, part]

    factors = [factor_ref[h] for h in range(heads)]

    unroll = diag.shape[0] * diag.shape[2] // (heads * width)

    @pl.loop(0, count // unroll)
    def _(group):
        spots = [pl.ds(group * unroll + u, cols, stride=rows) for u in range(unroll)]
        lines = []
        for at in spots:
            line = [normed.at[c][at, :].astype(jnp.bfloat16) for c in range(len(lanes))]
            line = jnp.concatenate(line, 1)
            if width > cols:
                line = jnp.concatenate([line, jnp.zeros((width - cols, features), jnp.bfloat16)], 0)
            lines.append(line)
        stack = jnp.concatenate(lines, 0)
        keys = dot(stack, wk_ref[...]).astype(jnp.bfloat16)
        both = dot(wqv_ref[...], stack, NT).astype(jnp.bfloat16)
        mixes = attend_lines(keys, both, factors, diag, wo_ref[...], cols, width, unroll)
        for u, at in enumerate(spots):
            mix = mixes[u * width : u * width + cols].astype(jnp.bfloat16).astype(jnp.float32)
            for c, part in enumerate(lanes):
                state.at[c][at, :] = state.at[c][at, :] + mix[:, part]

    near_count = o_refs[0].shape[1]
    for o_ref in o_refs:
        size = o_ref.shape[1]
        for i in range(bands):
            for j in range(blocks):
                if o_ref is o_refs[0]:
                    first = i * size + (0 if i < bands // 2 else part_cols - bands * size)
                else:
                    first = bands // 2 * near_count + i * size
                start = (j * part_cols + first) * rows
                at = slice(start, start + size * rows)
                y = jnp.concatenate([state[c, at, :] for c in range(len(lanes))], 1)
                o_ref[i * blocks + j] = y.reshape(size, rows, features).astype(jnp.bfloat16)


def lat_kernel(factor_ref, place_ref, x_ref, gain_ref, wk_ref, wqv_ref, wo_ref, *refs):
    *o_refs, state, diag = refs
    sources, _, rows, features = x_ref.shape
    length = sources * rows
    heads = factor_ref.shape[0]
    bands = len(o_refs)
    band = length // bands
    tall = o_refs[0].shape[1]

    @pl.when(pl.program_id(0) == 0)
    def _():
        diag[...] = jnp.zeros_like(diag)
        state[...] = jnp.zeros_like(state)

    x = x_ref[:, 0].astype(jnp.float32).reshape(length, features)
    line = layer_norm(x, gain_ref[...]).astype(jnp.bfloat16)
    keys = dot(line, wk_ref[...]).astype(jnp.bfloat16)
    both = dot(wqv_ref[...], line, NT).astype(jnp.bfloat16)
    factors = [factor_ref[h] for h in range(heads)]
    mix = attend_line(keys, both, factors, diag, wo_ref[...])
    state[MARGIN : MARGIN + length, :] = x + mix.astype(jnp.bfloat16).astype(jnp.float32)
    for k, o_ref in enumerate(o_refs):
        target = lax.rem(place_ref[0] + k, bands)
        at = pl.ds(pl.multiple_of(target * band, 8), tall)
        o_ref[0] = state[at, :].astype(jnp.bfloat16)


def edge_column(source, count, bands, cols):
    return source * count + jnp.where(source < bands // 2, 0, cols - bands * count)


def mixer_kernel(place_ref, *refs, kinds, outs, filled, tile):
    inputs = refs[: len(kinds)]
    taps_ref, gain_ref, win_ref, wdown_ref = refs[len(kinds) : len(kinds) + 4]
    o_ref, wide, normed, done, sems = refs[len(kinds) + 4 + filled :]
    cols, rows, features = o_ref.shape
    hidden_len = wdown_ref.shape[0]
    bands = sum(kind == "near" for kind, _ in kinds)
    near_count = inputs[0].shape[0]
    for (kind, k), piece in zip(kinds, inputs):
        count = piece.shape[0]
        source = lax.rem(place_ref[0] + (bands - k), bands) if kind != "fixed" else 0
        if kind == "near":
            column = edge_column(source, count, bands, cols)
        elif kind == "far":
            column = bands // 2 * near_count + source * count
        else:
            column = k
        wide[pl.ds(column + MARGIN, count)] = piece[...].astype(jnp.float32)

    def smooth(n):
        source = outs[n]
        total = None
        for dy in range(KERNEL):
            part = None
            for dx in range(KERNEL):
                tap = taps_ref[dy * KERNEL + dx : dy * KERNEL + dx + 1, :]
                term = wide[source + dx] * tap
                part = term if part is None else part + term
            part = part[dy : dy + rows]
            total = part if total is None else total + part
        normed[n * rows : (n + 1) * rows, :] = layer_norm(total, gain_ref[...]).astype(jnp.bfloat16)

    def mix(t, k):
        line = normed[t * tile * rows : (t + 1) * tile * rows, :]
        gate = dot(line, win_ref[:, k])
        up = dot(line, win_ref[:, slice(hidden_len + k.start, hidden_len + k.stop)])
        hidden = (0.5 * gate * (1.0 + jnp.tanh(0.5 * gate)) * up).astype(jnp.bfloat16)
        return dot(hidden, wdown_ref[k, :])

    for n in range(tile):
        smooth(n)
    chunk = hidden_len // tile
    copies = []
    for t in range(len(outs) // tile):
        update = None
        for n in range(tile):
            term = mix(t, slice(n * chunk, (n + 1) * chunk))
            update = term if update is None else update + term
            if (t + 1) * tile + n < len(outs):
                smooth((t + 1) * tile + n)
        for n in range(tile):
            target = outs[t * tile + n]
            kept = wide[target + MARGIN, MARGIN : MARGIN + rows, :]
            done[t * tile + n] = (kept + update[n * rows : (n + 1) * rows]).astype(jnp.bfloat16)
            copies.append(
                pltpu.make_async_copy(done.at[t * tile + n], o_ref.at[target], sems.at[t * tile + n])
            )
            copies[-1].start()
    for copy in copies:
        copy.wait()


def whole(shape):
    return pl.BlockSpec(shape, lambda *_: (0,) * len(shape))


def split_weights(qkv, features):
    keys = qkv[:, features : 2 * features]
    both = jnp.concatenate([qkv[:, :features], qkv[:, 2 * features :]], 1).T
    return keys, both


SMEM = pl.BlockSpec(memory_space=pltpu.SMEM)
VMEM = pl.BlockSpec(memory_space=pltpu.VMEM)


def cost(cells, length, features, heads):
    return pl.CostEstimate(
        flops=2 * cells * features * (4 * features + (heads + 2) * length),
        bytes_accessed=4 * cells * features,
        transcendentals=cells * length * heads,
    )


def params(*sizes):
    return pltpu.CompilerParams(vmem_limit_bytes=min(60 * 2**20, 2 * sum(sizes) + 2**22))


def lon_call(pieces, place, out, factors, gains, weights, out_w, bands, count, chunk, chunks, sizes):
    blocks = len(pieces)
    part_cols, rows, features = pieces[0].shape
    all_cols = blocks * part_cols
    heads = factors.shape[0]
    unroll = next(u for u in (8, 2, 1) if u == 1 or (count % u == 0 and all_cols <= 2 * LANES))
    some = pl.BlockSpec(memory_space=pl.ANY)
    return pl.pallas_call(
        functools.partial(lon_kernel, blocks=blocks, bands=bands, count=count, filled=len(out)),
        grid=(1,),
        out_shape=[
            jax.ShapeDtypeStruct((bands * blocks, size, chunks * rows, features), jnp.bfloat16)
            for size in sizes
        ],
        in_specs=[SMEM] * 2 + [VMEM] * (blocks + 4) + [some] * len(out),
        out_specs=[
            pl.BlockSpec((bands * blocks, size, rows, features), lambda _: (0, 0, chunk, 0))
            for size in sizes
        ],
        scratch_shapes=[
            pltpu.VMEM((features // LANES, all_cols * rows, LANES), jnp.float32),
            pltpu.VMEM((features // LANES, all_cols * rows, LANES), jnp.float32),
            pltpu.VMEM((heads * unroll // 2, features, 2 * padded(all_cols, LANES)), jnp.bfloat16),
        ],
        input_output_aliases={blocks + 6 + n: n for n in range(len(out))},
        cost_estimate=cost(all_cols * count, all_cols, features, heads),
        compiler_params=params(
            8 * all_cols * rows * features,
            2 * heads * unroll * features * padded(all_cols, LANES),
            4 * heads * unroll * all_cols * padded(all_cols, LANES),
        ),
        name="lon_attention",
    )(factors, place, *pieces, gains, *weights, out_w, *out)


def lat_call(columns, place, factors, gains, weights, out_w, bands):
    sources, count, rows, features = columns.shape
    heads = factors.shape[0]
    length = sources * rows
    tall = padded(length // bands + 2 * MARGIN, 8)
    return pl.pallas_call(
        lat_kernel,
        grid=(count,),
        out_shape=[jax.ShapeDtypeStruct((count, tall, features), jnp.bfloat16)] * bands,
        in_specs=[
            SMEM,
            SMEM,
            pl.BlockSpec((sources, 1, rows, features), lambda k: (0, k, 0, 0)),
            whole((1, features)),
            whole((features, features)),
            whole((2 * features, features)),
            whole((features, features)),
        ],
        out_specs=[pl.BlockSpec((1, tall, features), lambda k: (k, 0, 0))] * bands,
        scratch_shapes=[
            pltpu.VMEM((length - length // bands + tall, features), jnp.float32),
            pltpu.VMEM((heads // 2, features, 2 * length), jnp.bfloat16),
        ],
        cost_estimate=cost(count * length, length, features, heads),
        compiler_params=params(
            8 * length * features, 2 * heads * features * length, 4 * heads * length * length
        ),
        name="lat_attention",
    )(factors, place, columns, gains, *weights, out_w)


def mixer_call(place, near, far, fixed, outs, cols, rows, out, taps, gains, win, wdown):
    inputs = [*near, *far, *[piece for _, piece in fixed]]
    kinds = [("near", k) for k in range(len(near))] + [("far", k) for k in range(len(far))]
    kinds += [("fixed", column) for column, _ in fixed]
    _, tall, features = inputs[0].shape
    count = len(outs)
    tile = next(n for n in (4, 2, 1) if count % n == 0)
    some = pl.BlockSpec(memory_space=pl.ANY)
    before = [] if out is None else [out]
    return pl.pallas_call(
        functools.partial(mixer_kernel, kinds=kinds, outs=outs, filled=len(before), tile=tile),
        out_shape=jax.ShapeDtypeStruct((cols, rows, features), jnp.bfloat16),
        in_specs=[SMEM] + [VMEM] * (len(inputs) + 4) + [some] * len(before),
        out_specs=some,
        scratch_shapes=[
            pltpu.VMEM((cols + 2 * MARGIN, tall, features), jnp.float32),
            pltpu.VMEM((count * rows, features), jnp.bfloat16),
            pltpu.VMEM((count, rows, features), jnp.bfloat16),
            pltpu.SemaphoreType.DMA((count,)),
        ],
        input_output_aliases={len(inputs) + 5: 0} if before else {},
        cost_estimate=pl.CostEstimate(
            flops=2 * count * rows * features * 3 * wdown.shape[0],
            bytes_accessed=4 * count * rows * features,
            transcendentals=count * rows * wdown.shape[0],
        ),
        compiler_params=params(
            4 * (cols + 2 * MARGIN) * tall * features, 8 * tile * rows * wdown.shape[0]
        ),
        name="mixer",
    )(place, *inputs, taps, gains, win, wdown, *before)


def per_device(
    fields,
    norm_gains,
    lon_qkv,
    lon_out,
    lat_qkv,
    lat_out,
    logit_scales,
    conv_taps,
    mlp_in,
    mlp_down,
):
    lat_rows, lon_cols, features = fields.shape
    blocks = lax.axis_size("lon")
    bands = lax.axis_size("lat")
    sub_rows = lat_rows // blocks
    tall_rows = padded(sub_rows, 8)
    sub_cols = lon_cols // bands
    all_rows = lat_rows * bands
    tall = padded(lat_rows + 2 * MARGIN, 8)
    factors = logit_scales * LOG2E

    grid = jnp.transpose(fields, (1, 0, 2)).reshape(lon_cols, blocks, sub_rows, features)
    if tall_rows > sub_rows:
        grid = jnp.pad(grid, ((0, 0), (0, 0), (0, tall_rows - sub_rows), (0, 0)))
    grid = grid.reshape(lon_cols, blocks * tall_rows, features)
    place = lax.axis_index("lon").astype(jnp.int32)
    band = lax.axis_index("lat").astype(jnp.int32)
    chunks = tall_rows // 8
    sizes = [sub_cols - sub_cols // 2, sub_cols // 2]
    weights = split_weights(lon_qkv, features)
    moved = []
    for chunk in range(chunks):
        pieces = []
        for k in range(blocks):
            target = lax.rem(place + k, blocks)
            piece = lax.dynamic_slice_in_dim(grid, target * tall_rows + chunk * 8, 8, 1)
            if k:
                piece = lax.ppermute(piece, "lon", [(i, (i + k) % blocks) for i in range(blocks)])
            pieces.append(piece)
        moved.append(pieces)
    first_state = []
    for chunk, pieces in enumerate(moved):
        count = min(8, sub_rows - chunk * 8)
        first_state = lon_call(
            pieces,
            place.reshape(1),
            first_state,
            factors[0],
            norm_gains[0:1],
            weights,
            lon_out,
            bands,
            count,
            chunk,
            chunks,
            sizes,
        )

    def to_columns(state):
        columns = lax.all_to_all(state, ("lat", "lon"), split_axis=0, concat_axis=0, tiled=True)
        if tall_rows > sub_rows:
            columns = jnp.swapaxes(columns[:, :, :sub_rows], 0, 1)
            columns = columns.reshape(1, columns.shape[0], all_rows, features)
        return columns

    def to_block(pieces):
        return [
            lax.ppermute(piece, "lat", [(i, (i + k) % bands) for i in range(bands)]) if k else piece
            for k, piece in enumerate(pieces)
        ]

    weights = split_weights(lat_qkv, features)

    def attend(columns):
        return lat_call(
            columns, band.reshape(1), factors[1], norm_gains[1:2], weights, lat_out, bands
        )

    near, far = first_state
    near = to_columns(near)
    near, far = lax.optimization_barrier((near, far))
    far = to_columns(far)
    near = to_block(attend(near))
    near, far = lax.optimization_barrier((near, attend(far)))
    far = to_block(far)

    def pick(k, start, stop):
        chosen = near[0][start:stop]
        for n in range(1, bands):
            chosen = jnp.where(k == n, near[n][start:stop], chosen)
        return chosen

    up = [(i, (i + 1) % blocks) for i in range(blocks)]
    first = pick(band, 0, MARGIN)
    last = pick(lax.rem(band + 1, bands), sizes[0] - MARGIN, sizes[0])
    fixed = [
        (-MARGIN, lax.ppermute(last, "lon", up)),
        (lon_cols, lax.ppermute(first, "lon", [(j, i) for i, j in up])),
    ]
    mixer = (conv_taps, norm_gains[2:3], mlp_in, mlp_down)
    inner = range(bands // 2 * sizes[0] - MARGIN, lon_cols - bands // 2 * sizes[0] + MARGIN)
    outer = [c for c in range(lon_cols) if c not in inner]
    spot = band.reshape(1)
    out = mixer_call(spot, near, [], fixed, outer, lon_cols, lat_rows, None, *mixer)
    out = mixer_call(spot, near, far, [], list(inner), lon_cols, lat_rows, out, *mixer)
    return jnp.transpose(out, (1, 0, 2))


def solution(mesh):
    in_specs = (P(("groups", "lat"), "lon", None), P(), P(), P(), P(), P(), P(), P(), P(), P())
    out_specs = P(("groups", "lat"), "lon", None)
    return jax.shard_map(
        per_device, mesh=mesh, in_specs=in_specs, out_specs=out_specs, check_vma=False
    )
```

```python
import functools

import jax
import jax.numpy as jnp
from jax import lax
from jax.experimental import pallas as pl
from jax.experimental.pallas import tpu as pltpu
from jax.sharding import PartitionSpec as P

KERNEL = 5
MARGIN = KERNEL // 2
EPSILON = 1e-05
LOG2E = 1.4426950408889634
LANES = 128

NT = (((1,), (1,)), ((), ()))
TN = (((0,), (0,)), ((), ()))


def dot(a, b, dims=(((1,), (0,)), ((), ()))):
    return lax.dot_general(a, b, dims, preferred_element_type=jnp.float32)


def padded(n, unit):
    return -(-n // unit) * unit


def layer_norm(values, gains):
    average = jnp.mean(values, -1, keepdims=True)
    centred = values - average
    spread = jnp.mean(centred * centred, -1, keepdims=True)
    return centred * lax.rsqrt(spread + EPSILON) * gains


def attend_line(keys, both, factors, diag, out_w):
    length, features = keys.shape
    heads = len(factors)
    size = features // heads
    joined = diag.shape[2] // length
    for h in range(heads):
        rows = slice(h * size, (h + 1) * size)
        lane = h % joined * length
        diag[h // joined, rows, lane : lane + length] = both[rows]
    groups = heads // joined
    scores, rounded, total, parts = {}, {}, {}, []

    def soften(h):
        lane = h % joined * length
        score = scores[h // joined][:, lane : lane + length]
        top = jnp.max(score, 0, keepdims=True)
        weights = jnp.exp2((score - top) * factors[h])
        total[h] = jnp.sum(weights, 0, keepdims=True)
        rounded[h] = weights.astype(jnp.bfloat16)

    def gather(h):
        values = both[features + h * size : features + (h + 1) * size]
        parts.append((dot(values, rounded[h]) / total[h]).astype(jnp.bfloat16))

    for p in range(groups + 1 + 1):
        if p < groups:
            scores[p] = dot(keys, diag[p])
        if 0 <= p - 1 < groups:
            for h in range((p - 1) * joined, (p - 1 + 1) * joined):
                soften(h)
        if 0 <= p - 1 - 1 < groups:
            for h in range((p - 1 - 1) * joined, (p - 1 - 1 + 1) * joined):
                gather(h)
    return dot(jnp.concatenate(parts, 0), out_w, TN)


def attend_lines(keys, both, factors, diag, out_w, count, width, lines):
    features = keys.shape[1]
    heads = len(factors)
    size = features // heads
    joined = diag.shape[2] // width
    groups = heads // joined
    for u in range(lines):
        for h in range(heads):
            rows = slice(h * size, (h + 1) * size)
            lane = h % joined * width
            diag[u * groups + h // joined, rows, lane : lane + width] = both[rows, u * width : (u + 1) * width]
    scores = [
        [dot(keys[u * width : u * width + count], diag[u * groups + p]) for p in range(groups)]
        for u in range(lines)
    ]
    pairs = [(u, h) for u in range(lines) for h in range(heads)]
    rounded, total = {}, {}
    for u, h in pairs:
        lane = h % joined * width
        score = scores[u][h // joined][:, lane : lane + width]
        top = jnp.max(score, 0, keepdims=True)
        weights = jnp.exp2((score - top) * factors[h])
        total[u, h] = jnp.sum(weights, 0, keepdims=True)
        packed = weights.astype(jnp.bfloat16)
        if width > count:
            packed = jnp.concatenate([packed, jnp.zeros((width - count, width), jnp.bfloat16)], 0)
        rounded[u, h] = packed
    parts = {}
    for u, h in pairs:
        values = both[features + h * size : features + (h + 1) * size, u * width : (u + 1) * width]
        parts[u, h] = (dot(values, rounded[u, h]) / total[u, h]).astype(jnp.bfloat16)
    context = [jnp.concatenate([parts[u, h] for h in range(heads)], 0) for u in range(lines)]
    return dot(jnp.concatenate(context, 1), out_w, TN)


def lon_kernel(factor_ref, place_ref, *refs, blocks, bands, count, sizes):
    pieces = refs[:blocks]
    gain_ref, wk_ref, wqv_ref, wo_ref = refs[blocks : blocks + 4]
    *o_refs, state, normed, diag = refs[blocks + 4 :]
    part_cols, rows, features = pieces[0].shape
    cols = blocks * part_cols
    heads = factor_ref.shape[0]
    width = padded(cols, LANES)
    diag[...] = jnp.zeros_like(diag)
    lanes = [slice(c, c + LANES) for c in range(0, features, LANES)]
    for k, piece in enumerate(pieces):
        source = lax.rem(place_ref[0] + (blocks - k), blocks)
        x = piece[...].astype(jnp.float32).reshape(part_cols * rows, features)
        y = layer_norm(x, gain_ref[...])
        at = pl.ds(pl.multiple_of(source * (part_cols * rows), 8), part_cols * rows)
        for c, part in enumerate(lanes):
            state[c, at, :] = x[:, part]
            normed[c, at, :] = y[:, part]

    factors = [factor_ref[h] for h in range(heads)]

    unroll = diag.shape[0] * diag.shape[2] // (heads * width)

    @pl.loop(0, count // unroll)
    def _(group):
        spots = [pl.ds(group * unroll + u, cols, stride=rows) for u in range(unroll)]
        lines = []
        for at in spots:
            line = [normed.at[c][at, :].astype(jnp.bfloat16) for c in range(len(lanes))]
            line = jnp.concatenate(line, 1)
            if width > cols:
                line = jnp.concatenate([line, jnp.zeros((width - cols, features), jnp.bfloat16)], 0)
            lines.append(line)
        stack = jnp.concatenate(lines, 0)
        keys = dot(stack, wk_ref[...]).astype(jnp.bfloat16)
        both = dot(wqv_ref[...], stack, NT).astype(jnp.bfloat16)
        mixes = attend_lines(keys, both, factors, diag, wo_ref[...], cols, width, unroll)
        for u, at in enumerate(spots):
            mix = mixes[u * width : u * width + cols].astype(jnp.bfloat16).astype(jnp.float32)
            for c, part in enumerate(lanes):
                state.at[c][at, :] = state.at[c][at, :] + mix[:, part]

    for k, o_ref in enumerate(o_refs):
        target = lax.rem(place_ref[0] + k, blocks)
        at_out = 0
        for i in range(bands):
            near = i * sizes[0] + (0 if i < bands // 2 else part_cols - bands * sizes[0])
            for first, size in ((near, sizes[0]), (bands // 2 * sizes[0] + i * sizes[1], sizes[1])):
                start = (target * part_cols + first) * rows
                at = pl.ds(pl.multiple_of(start, 8), size * rows)
                y = jnp.concatenate([state[c, at, :] for c in range(len(lanes))], 1)
                y = y.reshape(size, rows, features).astype(jnp.bfloat16)
                o_ref[at_out : at_out + size] = y
                at_out += size


def lat_kernel(factor_ref, place_ref, *refs, bands):
    count = len(refs) - bands - 7
    inputs = refs[:count]
    gain_ref, wk_ref, wqv_ref, wo_ref = refs[count : count + 4]
    *o_refs, line_ref, state, diag = refs[count + 4 :]
    blocks, _, rows, features = inputs[0].shape
    length = line_ref.shape[0]
    heads = factor_ref.shape[0]
    band = length // bands
    tall = o_refs[0].shape[1]

    @pl.when(pl.program_id(0) == 0)
    def _():
        diag[...] = jnp.zeros_like(diag)
        state[...] = jnp.zeros_like(state)

    for n, x_ref in enumerate(inputs):
        source = lax.rem(place_ref[0] + (bands - n % bands), bands) if count > 1 else 0
        for m in range(blocks):
            block = lax.rem(place_ref[1] + (blocks - m), blocks) if count > 1 else 0
            start = source * band + block * (band // blocks) + n // bands * rows
            line_ref[pl.ds(pl.multiple_of(start, 8), rows), :] = x_ref[m, 0].astype(jnp.float32)
    x = line_ref[...]
    line = layer_norm(x, gain_ref[...]).astype(jnp.bfloat16)
    keys = dot(line, wk_ref[...]).astype(jnp.bfloat16)
    both = dot(wqv_ref[...], line, NT).astype(jnp.bfloat16)
    factors = [factor_ref[h] for h in range(heads)]
    mix = attend_line(keys, both, factors, diag, wo_ref[...])
    state[MARGIN : MARGIN + length, :] = x + mix.astype(jnp.bfloat16).astype(jnp.float32)
    for k, o_ref in enumerate(o_refs):
        target = lax.rem(place_ref[0] + k, bands)
        at = pl.ds(pl.multiple_of(target * band, 8), tall)
        o_ref[0] = state[at, :].astype(jnp.bfloat16)


def edge_column(source, count, bands, cols):
    return source * count + jnp.where(source < bands // 2, 0, cols - bands * count)


def mixer_kernel(place_ref, *refs, kinds, outs, filled, tile):
    inputs = refs[: len(kinds)]
    taps_ref, gain_ref, win_ref, wdown_ref = refs[len(kinds) : len(kinds) + 4]
    o_ref, wide, normed, done, sems = refs[len(kinds) + 4 + filled :]
    cols, rows, features = o_ref.shape
    hidden_len = wdown_ref.shape[0]
    bands = sum(kind == "near" for kind, _ in kinds)
    near_count = inputs[0].shape[0]
    for (kind, k), piece in zip(kinds, inputs):
        count = piece.shape[0]
        source = lax.rem(place_ref[0] + (bands - k), bands) if kind != "fixed" else 0
        if kind == "near":
            column = edge_column(source, count, bands, cols)
        elif kind == "far":
            column = bands // 2 * near_count + source * count
        else:
            column = k
        wide[pl.ds(column + MARGIN, count)] = piece[...].astype(jnp.float32)

    def smooth(n):
        source = outs[n]
        total = None
        for dy in range(KERNEL):
            part = None
            for dx in range(KERNEL):
                tap = taps_ref[dy * KERNEL + dx : dy * KERNEL + dx + 1, :]
                term = wide[source + dx] * tap
                part = term if part is None else part + term
            part = part[dy : dy + rows]
            total = part if total is None else total + part
        normed[n * rows : (n + 1) * rows, :] = layer_norm(total, gain_ref[...]).astype(jnp.bfloat16)

    def mix(t, k):
        line = normed[t * tile * rows : (t + 1) * tile * rows, :]
        gate = dot(line, win_ref[:, k])
        up = dot(line, win_ref[:, slice(hidden_len + k.start, hidden_len + k.stop)])
        hidden = (0.5 * gate * (1.0 + jnp.tanh(0.5 * gate)) * up).astype(jnp.bfloat16)
        return dot(hidden, wdown_ref[k, :])

    for n in range(tile):
        smooth(n)
    chunk = hidden_len // tile
    copies = []
    for t in range(len(outs) // tile):
        update = None
        for n in range(tile):
            term = mix(t, slice(n * chunk, (n + 1) * chunk))
            update = term if update is None else update + term
            if (t + 1) * tile + n < len(outs):
                smooth((t + 1) * tile + n)
        for n in range(tile):
            target = outs[t * tile + n]
            kept = wide[target + MARGIN, MARGIN : MARGIN + rows, :]
            done[t * tile + n] = (kept + update[n * rows : (n + 1) * rows]).astype(jnp.bfloat16)
            copies.append(
                pltpu.make_async_copy(done.at[t * tile + n], o_ref.at[target], sems.at[t * tile + n])
            )
            copies[-1].start()
    for copy in copies:
        copy.wait()


def whole(shape):
    return pl.BlockSpec(shape, lambda *_: (0,) * len(shape))


def split_weights(qkv, features):
    keys = qkv[:, features : 2 * features]
    both = jnp.concatenate([qkv[:, :features], qkv[:, 2 * features :]], 1).T
    return keys, both


SMEM = pl.BlockSpec(memory_space=pltpu.SMEM)
VMEM = pl.BlockSpec(memory_space=pltpu.VMEM)


def cost(cells, length, features, heads):
    return pl.CostEstimate(
        flops=2 * cells * features * (4 * features + (heads + 2) * length),
        bytes_accessed=4 * cells * features,
        transcendentals=cells * length * heads,
    )


def params(*sizes):
    return pltpu.CompilerParams(vmem_limit_bytes=min(60 * 2**20, 2 * sum(sizes) + 2**22))


def lon_call(pieces, place, factors, gains, weights, out_w, bands, count, sizes):
    blocks = len(pieces)
    part_cols, rows, features = pieces[0].shape
    all_cols = blocks * part_cols
    heads = factors.shape[0]
    unroll = next(u for u in (8, 2, 1) if u == 1 or (count % u == 0 and all_cols <= 2 * LANES))
    return pl.pallas_call(
        functools.partial(lon_kernel, blocks=blocks, bands=bands, count=count, sizes=sizes),
        out_shape=[jax.ShapeDtypeStruct((part_cols, rows, features), jnp.bfloat16)] * blocks,
        in_specs=[SMEM] * 2 + [VMEM] * (blocks + 4),
        out_specs=[VMEM] * blocks,
        scratch_shapes=[
            pltpu.VMEM((features // LANES, all_cols * rows, LANES), jnp.float32),
            pltpu.VMEM((features // LANES, all_cols * rows, LANES), jnp.float32),
            pltpu.VMEM((heads * unroll // 2, features, 2 * padded(all_cols, LANES)), jnp.bfloat16),
        ],
        cost_estimate=cost(all_cols * count, all_cols, features, heads),
        compiler_params=params(
            8 * all_cols * rows * features,
            2 * heads * unroll * features * padded(all_cols, LANES),
            4 * heads * unroll * all_cols * padded(all_cols, LANES),
        ),
        name="lon_attention",
    )(factors, place, *pieces, gains, *weights, out_w)


def lat_call(columns, first, count, place, factors, gains, weights, out_w, bands):
    blocks, _, rows, features = columns[0].shape
    heads = factors.shape[0]
    length = len(columns) * blocks * rows
    tall = padded(length // bands + 2 * MARGIN, 8)
    return pl.pallas_call(
        functools.partial(lat_kernel, bands=bands),
        grid=(count,),
        out_shape=[jax.ShapeDtypeStruct((count, tall, features), jnp.bfloat16)] * bands,
        in_specs=[
            SMEM,
            SMEM,
            *[pl.BlockSpec((blocks, 1, rows, features), lambda k: (0, k + first, 0, 0))] * len(columns),
            whole((1, features)),
            whole((features, features)),
            whole((2 * features, features)),
            whole((features, features)),
        ],
        out_specs=[pl.BlockSpec((1, tall, features), lambda k: (k, 0, 0))] * bands,
        scratch_shapes=[
            pltpu.VMEM((length, features), jnp.float32),
            pltpu.VMEM((length - length // bands + tall, features), jnp.float32),
            pltpu.VMEM((heads // 2, features, 2 * length), jnp.bfloat16),
        ],
        cost_estimate=cost(count * length, length, features, heads),
        compiler_params=params(
            12 * length * features, 2 * heads * features * length, 4 * heads * length * length
        ),
        name="lat_attention",
    )(factors, place, *columns, gains, *weights, out_w)


def mixer_call(place, near, far, fixed, outs, cols, rows, out, taps, gains, win, wdown):
    inputs = [*near, *far, *[piece for _, piece in fixed]]
    kinds = [("near", k) for k in range(len(near))] + [("far", k) for k in range(len(far))]
    kinds += [("fixed", column) for column, _ in fixed]
    _, tall, features = inputs[0].shape
    count = len(outs)
    tile = next(n for n in (4, 2, 1) if count % n == 0)
    some = pl.BlockSpec(memory_space=pl.ANY)
    before = [] if out is None else [out]
    return pl.pallas_call(
        functools.partial(mixer_kernel, kinds=kinds, outs=outs, filled=len(before), tile=tile),
        out_shape=jax.ShapeDtypeStruct((cols, rows, features), jnp.bfloat16),
        in_specs=[SMEM] + [VMEM] * (len(inputs) + 4) + [some] * len(before),
        out_specs=some,
        scratch_shapes=[
            pltpu.VMEM((cols + 2 * MARGIN, tall, features), jnp.float32),
            pltpu.VMEM((count * rows, features), jnp.bfloat16),
            pltpu.VMEM((count, rows, features), jnp.bfloat16),
            pltpu.SemaphoreType.DMA((count,)),
        ],
        input_output_aliases={len(inputs) + 5: 0} if before else {},
        cost_estimate=pl.CostEstimate(
            flops=2 * count * rows * features * 3 * wdown.shape[0],
            bytes_accessed=4 * count * rows * features,
            transcendentals=count * rows * wdown.shape[0],
        ),
        compiler_params=params(
            4 * (cols + 2 * MARGIN) * tall * features, 8 * tile * rows * wdown.shape[0]
        ),
        name="mixer",
    )(place, *inputs, taps, gains, win, wdown, *before)


def per_device(
    fields,
    norm_gains,
    lon_qkv,
    lon_out,
    lat_qkv,
    lat_out,
    logit_scales,
    conv_taps,
    mlp_in,
    mlp_down,
):
    lat_rows, lon_cols, features = fields.shape
    blocks = lax.axis_size("lon")
    bands = lax.axis_size("lat")
    sub_rows = lat_rows // blocks
    tall_rows = padded(sub_rows, 8)
    sub_cols = lon_cols // bands
    factors = logit_scales * LOG2E

    grid = jnp.transpose(fields, (1, 0, 2)).reshape(lon_cols, blocks, sub_rows, features)
    if tall_rows > sub_rows:
        grid = jnp.pad(grid, ((0, 0), (0, 0), (0, tall_rows - sub_rows), (0, 0)))
    grid = grid.reshape(lon_cols, blocks * tall_rows, features)
    place = lax.axis_index("lon").astype(jnp.int32)
    band = lax.axis_index("lat").astype(jnp.int32)
    chunks = tall_rows // 8
    sizes = [sub_cols - sub_cols // 2, sub_cols // 2]
    weights = split_weights(lon_qkv, features)
    def along(pieces, axis, count):
        return [
            lax.ppermute(piece, axis, [(i, (i + k) % count) for i in range(count)]) if k else piece
            for k, piece in enumerate(pieces)
        ]

    moved = []
    for chunk in range(chunks):
        pieces = []
        for k in range(blocks):
            target = lax.rem(place + k, blocks)
            pieces.append(lax.dynamic_slice_in_dim(grid, target * tall_rows + chunk * 8, 8, 1))
        moved.append(along(pieces, "lon", blocks))
    columns = []
    for chunk, pieces in enumerate(moved):
        count = min(8, sub_rows - chunk * 8)
        pieces = lon_call(
            pieces,
            place.reshape(1),
            factors[0],
            norm_gains[0:1],
            weights,
            lon_out,
            bands,
            count,
            sizes,
        )
        pieces = along(pieces, "lon", blocks)
        parts = []
        for k in range(bands):
            target = lax.rem(band + k, bands)
            parts.append(
                jnp.stack([lax.dynamic_slice_in_dim(p, target * sub_cols, sub_cols, 0) for p in pieces])
            )
        columns += along(parts, "lat", bands)
    if tall_rows > sub_rows:
        order = lax.rem(place + blocks - jnp.arange(blocks), blocks)
        columns = [
            jnp.swapaxes(jnp.take(part, order, 0)[:, :, :sub_rows], 0, 1).reshape(
                1, sub_cols, lat_rows, features
            )
            for part in columns
        ]
        order = lax.rem(band + bands - jnp.arange(bands), bands)
        columns = jnp.take(jnp.concatenate(columns), order, 0)
        columns = [jnp.swapaxes(columns, 0, 1).reshape(1, sub_cols, lat_rows * bands, features)]

    weights = split_weights(lat_qkv, features)

    def attend(first, count):
        spot = jnp.stack([band, place])
        return lat_call(
            columns, first, count, spot, factors[1], norm_gains[1:2], weights, lat_out, bands
        )

    near = along(attend(0, sizes[0]), "lat", bands)
    near, far = lax.optimization_barrier((near, attend(sizes[0], sizes[1])))
    far = along(far, "lat", bands)

    def pick(k, start, stop):
        chosen = near[0][start:stop]
        for n in range(1, bands):
            chosen = jnp.where(k == n, near[n][start:stop], chosen)
        return chosen

    up = [(i, (i + 1) % blocks) for i in range(blocks)]
    first = pick(band, 0, MARGIN)
    last = pick(lax.rem(band + 1, bands), sizes[0] - MARGIN, sizes[0])
    fixed = [
        (-MARGIN, lax.ppermute(last, "lon", up)),
        (lon_cols, lax.ppermute(first, "lon", [(j, i) for i, j in up])),
    ]
    mixer = (conv_taps, norm_gains[2:3], mlp_in, mlp_down)
    side = bands // 2 * sizes[0]
    ready = [*range(MARGIN, side - MARGIN), *range(lon_cols - side + MARGIN, lon_cols - MARGIN)]
    late = [c for c in range(lon_cols) if c not in ready]
    spot = band.reshape(1)
    out = mixer_call(spot, near, [], [], ready, lon_cols, lat_rows, None, *mixer)
    out = mixer_call(spot, near, far, fixed, late, lon_cols, lat_rows, out, *mixer)
    return jnp.transpose(out, (1, 0, 2))


def solution(mesh):
    in_specs = (P(("groups", "lat"), "lon", None), P(), P(), P(), P(), P(), P(), P(), P(), P())
    out_specs = P(("groups", "lat"), "lon", None)
    return jax.shard_map(
        per_device, mesh=mesh, in_specs=in_specs, out_specs=out_specs, check_vma=False
    )
```

```python
import functools

import jax
import jax.numpy as jnp
from jax import lax
from jax.experimental import pallas as pl
from jax.experimental.pallas import tpu as pltpu
from jax.sharding import PartitionSpec as P

KERNEL = 5
MARGIN = KERNEL // 2
EPSILON = 1e-05
LOG2E = 1.4426950408889634
LANES = 128

NT = (((1,), (1,)), ((), ()))
TN = (((0,), (0,)), ((), ()))


def dot(a, b, dims=(((1,), (0,)), ((), ()))):
    return lax.dot_general(a, b, dims, preferred_element_type=jnp.float32)


def padded(n, unit):
    return -(-n // unit) * unit


def layer_norm(values, gains):
    average = jnp.mean(values, -1, keepdims=True)
    centred = values - average
    spread = jnp.mean(centred * centred, -1, keepdims=True)
    return centred * lax.rsqrt(spread + EPSILON) * gains


def attend_columns(keys, both, factors, diag, out_w):
    length, features = keys[0].shape
    heads = len(factors)
    size = features // heads
    joined = diag.shape[3] // length
    groups = heads // joined
    for u in range(len(keys)):
        for h in range(heads):
            rows = slice(h * size, (h + 1) * size)
            lane = h % joined * length
            diag[u, h // joined, rows, lane : lane + length] = both[u][rows]
    scores, rounded, total = {}, {}, {}
    parts = [[] for _ in keys]

    def soften(u, h):
        lane = h % joined * length
        score = scores[u, h // joined][:, lane : lane + length]
        top = jnp.max(score, 0, keepdims=True)
        weights = jnp.exp2((score - top) * factors[h])
        total[u, h] = jnp.sum(weights, 0, keepdims=True)
        rounded[u, h] = weights.astype(jnp.bfloat16)

    def gather(u, h):
        values = both[u][features + h * size : features + (h + 1) * size]
        parts[u].append((dot(values, rounded[u, h]) / total[u, h]).astype(jnp.bfloat16))

    units = [(u, p) for p in range(groups) for u in range(len(keys))]
    for n in range(len(units) + 2):
        if n < len(units):
            u, p = units[n]
            scores[u, p] = dot(keys[u], diag[u, p])
        for act, lag in ((soften, 1), (gather, 2)):
            if 0 <= n - lag < len(units):
                u, p = units[n - lag]
                for h in range(p * joined, (p + 1) * joined):
                    act(u, h)
    return [dot(jnp.concatenate(part, 0), out_w, TN) for part in parts]


def attend_lines(keys, both, factors, diag, out_w, count, width, lines):
    features = keys.shape[1]
    heads = len(factors)
    size = features // heads
    joined = diag.shape[2] // width
    groups = heads // joined
    for u in range(lines):
        for h in range(heads):
            rows = slice(h * size, (h + 1) * size)
            lane = h % joined * width
            diag[u * groups + h // joined, rows, lane : lane + width] = both[rows, u * width : (u + 1) * width]
    scores = [
        [dot(keys[u * width : u * width + count], diag[u * groups + p]) for p in range(groups)]
        for u in range(lines)
    ]
    pairs = [(u, h) for u in range(lines) for h in range(heads)]
    rounded, total = {}, {}
    for u, h in pairs:
        lane = h % joined * width
        score = scores[u][h // joined][:, lane : lane + width]
        top = jnp.max(score, 0, keepdims=True)
        weights = jnp.exp2((score - top) * factors[h])
        total[u, h] = jnp.sum(weights, 0, keepdims=True)
        packed = weights.astype(jnp.bfloat16)
        if width > count:
            packed = jnp.concatenate([packed, jnp.zeros((width - count, width), jnp.bfloat16)], 0)
        rounded[u, h] = packed
    parts = {}
    for u, h in pairs:
        values = both[features + h * size : features + (h + 1) * size, u * width : (u + 1) * width]
        parts[u, h] = (dot(values, rounded[u, h]) / total[u, h]).astype(jnp.bfloat16)
    context = [jnp.concatenate([parts[u, h] for h in range(heads)], 0) for u in range(lines)]
    return dot(jnp.concatenate(context, 1), out_w, TN)


def lon_kernel(factor_ref, place_ref, *refs, blocks, bands, count, sizes):
    pieces = refs[:blocks]
    gain_ref, wk_ref, wqv_ref, wo_ref = refs[blocks : blocks + 4]
    *o_refs, state, normed, diag = refs[blocks + 4 :]
    part_cols, rows, features = pieces[0].shape
    cols = blocks * part_cols
    heads = factor_ref.shape[0]
    width = padded(cols, LANES)
    diag[...] = jnp.zeros_like(diag)
    lanes = [slice(c, c + LANES) for c in range(0, features, LANES)]
    for k, piece in enumerate(pieces):
        source = lax.rem(place_ref[0] + (blocks - k), blocks)
        x = piece[...].astype(jnp.float32).reshape(part_cols * rows, features)
        y = layer_norm(x, gain_ref[...])
        at = pl.ds(pl.multiple_of(source * (part_cols * rows), 8), part_cols * rows)
        for c, part in enumerate(lanes):
            state[c, at, :] = x[:, part]
            normed[c, at, :] = y[:, part]

    factors = [factor_ref[h] for h in range(heads)]

    unroll = diag.shape[0] * diag.shape[2] // (heads * width)

    @pl.loop(0, count // unroll)
    def _(group):
        spots = [pl.ds(group * unroll + u, cols, stride=rows) for u in range(unroll)]
        lines = []
        for at in spots:
            line = [normed.at[c][at, :].astype(jnp.bfloat16) for c in range(len(lanes))]
            line = jnp.concatenate(line, 1)
            if width > cols:
                line = jnp.concatenate([line, jnp.zeros((width - cols, features), jnp.bfloat16)], 0)
            lines.append(line)
        stack = jnp.concatenate(lines, 0)
        keys = dot(stack, wk_ref[...]).astype(jnp.bfloat16)
        both = dot(wqv_ref[...], stack, NT).astype(jnp.bfloat16)
        mixes = attend_lines(keys, both, factors, diag, wo_ref[...], cols, width, unroll)
        for u, at in enumerate(spots):
            mix = mixes[u * width : u * width + cols].astype(jnp.bfloat16).astype(jnp.float32)
            for c, part in enumerate(lanes):
                state.at[c][at, :] = state.at[c][at, :] + mix[:, part]

    for k, o_ref in enumerate(o_refs):
        target = lax.rem(place_ref[0] + k, blocks)
        at_out = 0
        for i in range(bands):
            near = i * sizes[0] + (0 if i < bands // 2 else part_cols - bands * sizes[0])
            for first, size in ((near, sizes[0]), (bands // 2 * sizes[0] + i * sizes[1], sizes[1])):
                start = (target * part_cols + first) * rows
                at = pl.ds(pl.multiple_of(start, 8), size * rows)
                y = jnp.concatenate([state[c, at, :] for c in range(len(lanes))], 1)
                y = y.reshape(size, rows, features).astype(jnp.bfloat16)
                o_ref[at_out : at_out + size] = y
                at_out += size


def lat_kernel(factor_ref, place_ref, *refs, bands, offset):
    count = len(refs) - bands - 7
    inputs = refs[:count]
    gain_ref, wk_ref, wqv_ref, wo_ref = refs[count : count + 4]
    *o_refs, line_ref, state, diag = refs[count + 4 :]
    blocks, _, rows, features = inputs[0].shape
    length = line_ref.shape[1]
    heads = factor_ref.shape[0]
    band = length // bands
    tall = o_refs[0].shape[1]

    @pl.when(pl.program_id(0) == 0)
    def _():
        diag[...] = jnp.zeros_like(diag)
        state[...] = jnp.zeros_like(state)

    cols = range(o_refs[0].shape[0])
    for n, x_ref in enumerate(inputs):
        source = lax.rem(place_ref[0] + (bands - n % bands), bands) if count > 1 else 0
        for m in range(blocks):
            block = lax.rem(place_ref[1] + (blocks - m), blocks) if count > 1 else 0
            start = source * band + block * (band // blocks) + n // bands * rows
            for u in cols:
                line_ref[u, pl.ds(pl.multiple_of(start, 8), rows), :] = x_ref[m, offset + u].astype(jnp.float32)
    lines = [layer_norm(line_ref[u], gain_ref[...]).astype(jnp.bfloat16) for u in cols]
    keys = [dot(line, wk_ref[...]).astype(jnp.bfloat16) for line in lines]
    both = [dot(wqv_ref[...], line, NT).astype(jnp.bfloat16) for line in lines]
    factors = [factor_ref[h] for h in range(heads)]
    mixes = attend_columns(keys, both, factors, diag, wo_ref[...])
    for u in cols:
        mix = mixes[u].astype(jnp.bfloat16).astype(jnp.float32)
        state[u, MARGIN : MARGIN + length, :] = line_ref[u] + mix
    for k, o_ref in enumerate(o_refs):
        target = lax.rem(place_ref[0] + k, bands)
        at = pl.ds(pl.multiple_of(target * band, 8), tall)
        for u in cols:
            o_ref[u] = state[u, at, :].astype(jnp.bfloat16)


def edge_column(source, count, bands, cols):
    return source * count + jnp.where(source < bands // 2, 0, cols - bands * count)


def mixer_kernel(place_ref, *refs, kinds, outs, filled, tile):
    inputs = refs[: len(kinds)]
    taps_ref, gain_ref, win_ref, wdown_ref = refs[len(kinds) : len(kinds) + 4]
    o_ref, wide, normed, done, sems = refs[len(kinds) + 4 + filled :]
    cols, rows, features = o_ref.shape
    hidden_len = wdown_ref.shape[0]
    bands = sum(kind == "near" for kind, _ in kinds)
    near_count = inputs[0].shape[0]
    for (kind, k), piece in zip(kinds, inputs):
        count = piece.shape[0]
        source = lax.rem(place_ref[0] + (bands - k), bands) if kind != "fixed" else 0
        if kind == "near":
            column = edge_column(source, count, bands, cols)
        elif kind == "far":
            column = bands // 2 * near_count + source * count
        else:
            column = k
        wide[pl.ds(column + MARGIN, count)] = piece[...].astype(jnp.float32)

    def smooth(n):
        source = outs[n]
        total = None
        for dy in range(KERNEL):
            part = None
            for dx in range(KERNEL):
                tap = taps_ref[dy * KERNEL + dx : dy * KERNEL + dx + 1, :]
                term = wide[source + dx] * tap
                part = term if part is None else part + term
            part = part[dy : dy + rows]
            total = part if total is None else total + part
        normed[n * rows : (n + 1) * rows, :] = layer_norm(total, gain_ref[...]).astype(jnp.bfloat16)

    def raise_up(t, k):
        line = normed[t * tile * rows : (t + 1) * tile * rows, :]
        gate = dot(line, win_ref[:, k])
        up = dot(line, win_ref[:, slice(hidden_len + k.start, hidden_len + k.stop)])
        return gate, up

    def bring_down(pair, k):
        gate, up = pair
        hidden = (0.5 * gate * (1.0 + jnp.tanh(0.5 * gate)) * up).astype(jnp.bfloat16)
        return dot(hidden, wdown_ref[k, :])

    for n in range(tile):
        smooth(n)
    chunk = hidden_len // tile
    copies = []
    for t in range(len(outs) // tile):
        update = None
        keys = [slice(n * chunk, (n + 1) * chunk) for n in range(tile)]
        pair = raise_up(t, keys[0])
        for n in range(tile):
            after = raise_up(t, keys[n + 1]) if n + 1 < tile else None
            if (t + 1) * tile + n < len(outs):
                smooth((t + 1) * tile + n)
            term = bring_down(pair, keys[n])
            pair = after
            update = term if update is None else update + term
        for n in range(tile):
            target = outs[t * tile + n]
            kept = wide[target + MARGIN, MARGIN : MARGIN + rows, :]
            done[t * tile + n] = (kept + update[n * rows : (n + 1) * rows]).astype(jnp.bfloat16)
            copies.append(
                pltpu.make_async_copy(done.at[t * tile + n], o_ref.at[target], sems.at[t * tile + n])
            )
            copies[-1].start()
    for copy in copies:
        copy.wait()


def whole(shape):
    return pl.BlockSpec(shape, lambda *_: (0,) * len(shape))


def split_weights(qkv, features):
    keys = qkv[:, features : 2 * features]
    both = jnp.concatenate([qkv[:, :features], qkv[:, 2 * features :]], 1).T
    return keys, both


SMEM = pl.BlockSpec(memory_space=pltpu.SMEM)
VMEM = pl.BlockSpec(memory_space=pltpu.VMEM)


def cost(cells, length, features, heads):
    return pl.CostEstimate(
        flops=2 * cells * features * (4 * features + (heads + 2) * length),
        bytes_accessed=4 * cells * features,
        transcendentals=cells * length * heads,
    )


def params(*sizes):
    return pltpu.CompilerParams(vmem_limit_bytes=min(60 * 2**20, 2 * sum(sizes) + 2**22))


def lon_call(pieces, place, factors, gains, weights, out_w, bands, count, sizes):
    blocks = len(pieces)
    part_cols, rows, features = pieces[0].shape
    all_cols = blocks * part_cols
    heads = factors.shape[0]
    unroll = next(u for u in (8, 2, 1) if u == 1 or (count % u == 0 and all_cols <= 2 * LANES))
    return pl.pallas_call(
        functools.partial(lon_kernel, blocks=blocks, bands=bands, count=count, sizes=sizes),
        out_shape=[jax.ShapeDtypeStruct((part_cols, rows, features), jnp.bfloat16)] * blocks,
        in_specs=[SMEM] * 2 + [VMEM] * (blocks + 4),
        out_specs=[VMEM] * blocks,
        scratch_shapes=[
            pltpu.VMEM((features // LANES, all_cols * rows, LANES), jnp.float32),
            pltpu.VMEM((features // LANES, all_cols * rows, LANES), jnp.float32),
            pltpu.VMEM((heads * unroll // 2, features, 2 * padded(all_cols, LANES)), jnp.bfloat16),
        ],
        cost_estimate=cost(all_cols * count, all_cols, features, heads),
        compiler_params=params(
            8 * all_cols * rows * features,
            2 * heads * unroll * features * padded(all_cols, LANES),
            4 * heads * unroll * all_cols * padded(all_cols, LANES),
        ),
        name="lon_attention",
    )(factors, place, *pieces, gains, *weights, out_w)


def lat_call(columns, first, count, place, factors, gains, weights, out_w, bands):
    blocks, _, rows, features = columns[0].shape
    heads = factors.shape[0]
    length = len(columns) * blocks * rows
    tall = padded(length // bands + 2 * MARGIN, 8)
    per = next(n for n in (2, 3, 1) if count % n == 0)
    offset = first if per == count else 0
    held = columns[0].shape[1] if per == count else per
    return pl.pallas_call(
        functools.partial(lat_kernel, bands=bands, offset=offset),
        grid=(count // per,),
        out_shape=[jax.ShapeDtypeStruct((count, tall, features), jnp.bfloat16)] * bands,
        in_specs=[
            SMEM,
            SMEM,
            *[pl.BlockSpec((blocks, held, rows, features), lambda k: (0, k + (first - offset) // per, 0, 0))]
            * len(columns),
            whole((1, features)),
            whole((features, features)),
            whole((2 * features, features)),
            whole((features, features)),
        ],
        out_specs=[pl.BlockSpec((per, tall, features), lambda k: (k, 0, 0))] * bands,
        scratch_shapes=[
            pltpu.VMEM((per, length, features), jnp.float32),
            pltpu.VMEM((per, length - length // bands + tall, features), jnp.float32),
            pltpu.VMEM((per, heads // 2, features, 2 * length), jnp.bfloat16),
        ],
        cost_estimate=cost(count * length, length, features, heads),
        compiler_params=params(
            12 * per * length * features,
            2 * per * heads * features * length,
            4 * heads * length * length,
        ),
        name="lat_attention",
    )(factors, place, *columns, gains, *weights, out_w)


def mixer_call(place, near, far, fixed, outs, cols, rows, out, taps, gains, win, wdown):
    inputs = [*near, *far, *[piece for _, piece in fixed]]
    kinds = [("near", k) for k in range(len(near))] + [("far", k) for k in range(len(far))]
    kinds += [("fixed", column) for column, _ in fixed]
    _, tall, features = inputs[0].shape
    count = len(outs)
    tile = next(n for n in (4, 2, 1) if count % n == 0)
    some = pl.BlockSpec(memory_space=pl.ANY)
    before = [] if out is None else [out]
    return pl.pallas_call(
        functools.partial(mixer_kernel, kinds=kinds, outs=outs, filled=len(before), tile=tile),
        out_shape=jax.ShapeDtypeStruct((cols, rows, features), jnp.bfloat16),
        in_specs=[SMEM] + [VMEM] * (len(inputs) + 4) + [some] * len(before),
        out_specs=some,
        scratch_shapes=[
            pltpu.VMEM((cols + 2 * MARGIN, tall, features), jnp.float32),
            pltpu.VMEM((count * rows, features), jnp.bfloat16),
            pltpu.VMEM((count, rows, features), jnp.bfloat16),
            pltpu.SemaphoreType.DMA((count,)),
        ],
        input_output_aliases={len(inputs) + 5: 0} if before else {},
        cost_estimate=pl.CostEstimate(
            flops=2 * count * rows * features * 3 * wdown.shape[0],
            bytes_accessed=4 * count * rows * features,
            transcendentals=count * rows * wdown.shape[0],
        ),
        compiler_params=params(
            4 * (cols + 2 * MARGIN) * tall * features, 8 * tile * rows * wdown.shape[0]
        ),
        name="mixer",
    )(place, *inputs, taps, gains, win, wdown, *before)


def per_device(
    fields,
    norm_gains,
    lon_qkv,
    lon_out,
    lat_qkv,
    lat_out,
    logit_scales,
    conv_taps,
    mlp_in,
    mlp_down,
):
    lat_rows, lon_cols, features = fields.shape
    blocks = lax.axis_size("lon")
    bands = lax.axis_size("lat")
    sub_rows = lat_rows // blocks
    tall_rows = padded(sub_rows, 8)
    sub_cols = lon_cols // bands
    factors = logit_scales * LOG2E

    grid = jnp.transpose(fields, (1, 0, 2)).reshape(lon_cols, blocks, sub_rows, features)
    if tall_rows > sub_rows:
        grid = jnp.pad(grid, ((0, 0), (0, 0), (0, tall_rows - sub_rows), (0, 0)))
    grid = grid.reshape(lon_cols, blocks * tall_rows, features)
    place = lax.axis_index("lon").astype(jnp.int32)
    band = lax.axis_index("lat").astype(jnp.int32)
    chunks = tall_rows // 8
    sizes = [sub_cols - sub_cols // 2, sub_cols // 2]
    weights = split_weights(lon_qkv, features)
    def along(pieces, axis, count):
        return [
            lax.ppermute(piece, axis, [(i, (i + k) % count) for i in range(count)]) if k else piece
            for k, piece in enumerate(pieces)
        ]

    moved = []
    for chunk in range(chunks):
        pieces = []
        for k in range(blocks):
            target = lax.rem(place + k, blocks)
            pieces.append(lax.dynamic_slice_in_dim(grid, target * tall_rows + chunk * 8, 8, 1))
        grid, pieces = lax.optimization_barrier((grid, pieces))
        moved.append(along(pieces, "lon", blocks))
    columns = []
    for chunk, pieces in enumerate(moved):
        count = min(8, sub_rows - chunk * 8)
        pieces = lon_call(
            pieces,
            place.reshape(1),
            factors[0],
            norm_gains[0:1],
            weights,
            lon_out,
            bands,
            count,
            sizes,
        )
        pieces = along(pieces, "lon", blocks)
        parts = []
        for k in range(bands):
            target = lax.rem(band + k, bands)
            parts.append(
                jnp.stack([lax.dynamic_slice_in_dim(p, target * sub_cols, sub_cols, 0) for p in pieces])
            )
        columns += along(parts, "lat", bands)
    if tall_rows > sub_rows:
        order = lax.rem(place + blocks - jnp.arange(blocks), blocks)
        columns = [
            jnp.swapaxes(jnp.take(part, order, 0)[:, :, :sub_rows], 0, 1).reshape(
                1, sub_cols, lat_rows, features
            )
            for part in columns
        ]
        order = lax.rem(band + bands - jnp.arange(bands), bands)
        columns = jnp.take(jnp.concatenate(columns), order, 0)
        columns = [jnp.swapaxes(columns, 0, 1).reshape(1, sub_cols, lat_rows * bands, features)]

    weights = split_weights(lat_qkv, features)

    def attend(first, count):
        spot = jnp.stack([band, place])
        return lat_call(
            columns, first, count, spot, factors[1], norm_gains[1:2], weights, lat_out, bands
        )

    near = along(attend(0, sizes[0]), "lat", bands)
    near, far = lax.optimization_barrier((near, attend(sizes[0], sizes[1])))
    far = along(far, "lat", bands)

    def pick(k, start, stop):
        chosen = near[0][start:stop]
        for n in range(1, bands):
            chosen = jnp.where(k == n, near[n][start:stop], chosen)
        return chosen

    up = [(i, (i + 1) % blocks) for i in range(blocks)]
    first = pick(band, 0, MARGIN)
    last = pick(lax.rem(band + 1, bands), sizes[0] - MARGIN, sizes[0])
    fixed = [
        (-MARGIN, lax.ppermute(last, "lon", up)),
        (lon_cols, lax.ppermute(first, "lon", [(j, i) for i, j in up])),
    ]
    mixer = (conv_taps, norm_gains[2:3], mlp_in, mlp_down)
    side = bands // 2 * sizes[0]
    ready = [*range(MARGIN, side - MARGIN), *range(lon_cols - side + MARGIN, lon_cols - MARGIN)]
    late = [c for c in range(lon_cols) if c not in ready]
    spot = band.reshape(1)
    out = mixer_call(spot, near, [], [], ready, lon_cols, lat_rows, None, *mixer)
    out = mixer_call(spot, near, far, fixed, late, lon_cols, lat_rows, out, *mixer)
    return jnp.transpose(out, (1, 0, 2))


def solution(mesh):
    in_specs = (P(("groups", "lat"), "lon", None), P(), P(), P(), P(), P(), P(), P(), P(), P())
    out_specs = P(("groups", "lat"), "lon", None)
    return jax.shard_map(
        per_device, mesh=mesh, in_specs=in_specs, out_specs=out_specs, check_vma=False
    )
```

```python
import functools

import jax
import jax.numpy as jnp
from jax import lax
from jax.experimental import pallas as pl
from jax.experimental.pallas import tpu as pltpu
from jax.sharding import PartitionSpec as P

KERNEL = 5
MARGIN = KERNEL // 2
EPSILON = 1e-05
LOG2E = 1.4426950408889634
LANES = 128

NT = (((1,), (1,)), ((), ()))
TN = (((0,), (0,)), ((), ()))


def dot(a, b, dims=(((1,), (0,)), ((), ()))):
    return lax.dot_general(a, b, dims, preferred_element_type=jnp.float32)


def padded(n, unit):
    return -(-n // unit) * unit


def layer_norm(values, gains):
    average = jnp.mean(values, -1, keepdims=True)
    centred = values - average
    spread = jnp.mean(centred * centred, -1, keepdims=True)
    return centred * lax.rsqrt(spread + EPSILON) * gains


def attend_columns(keys, both, factors, diag, out_w):
    length, features = keys[0].shape
    heads = len(factors)
    size = features // heads
    joined = diag.shape[3] // length
    groups = heads // joined
    for u in range(len(keys)):
        for h in range(heads):
            rows = slice(h * size, (h + 1) * size)
            lane = h % joined * length
            diag[u, h // joined, rows, lane : lane + length] = both[u][rows]
    scores, rounded, total = {}, {}, {}
    parts = [[] for _ in keys]

    def soften(u, h):
        lane = h % joined * length
        score = scores[u, h // joined][:, lane : lane + length]
        top = jnp.max(score, 0, keepdims=True)
        weights = jnp.exp2((score - top) * factors[h])
        total[u, h] = jnp.sum(weights, 0, keepdims=True)
        rounded[u, h] = weights.astype(jnp.bfloat16)

    def gather(u, h):
        values = both[u][features + h * size : features + (h + 1) * size]
        parts[u].append((dot(values, rounded[u, h]) * (1.0 / total[u, h])).astype(jnp.bfloat16))

    units = [(u, p) for p in range(groups) for u in range(len(keys))]
    for n in range(len(units) + 2):
        if n < len(units):
            u, p = units[n]
            scores[u, p] = dot(keys[u], diag[u, p])
        for act, lag in ((soften, 1), (gather, 2)):
            if 0 <= n - lag < len(units):
                u, p = units[n - lag]
                for h in range(p * joined, (p + 1) * joined):
                    act(u, h)
    return [dot(jnp.concatenate(part, 0), out_w, TN) for part in parts]


def attend_lines(keys, both, factors, diag, out_w, count, width, lines):
    features = keys.shape[1]
    heads = len(factors)
    size = features // heads
    joined = diag.shape[2] // width
    groups = heads // joined
    for u in range(lines):
        for h in range(heads):
            rows = slice(h * size, (h + 1) * size)
            lane = h % joined * width
            diag[u * groups + h // joined, rows, lane : lane + width] = both[rows, u * width : (u + 1) * width]
    scores = [
        [dot(keys[u * width : u * width + count], diag[u * groups + p]) for p in range(groups)]
        for u in range(lines)
    ]
    pairs = [(u, h) for u in range(lines) for h in range(heads)]
    rounded, total = {}, {}
    for u, h in pairs:
        lane = h % joined * width
        score = scores[u][h // joined][:, lane : lane + width]
        top = jnp.max(score, 0, keepdims=True)
        weights = jnp.exp2((score - top) * factors[h])
        total[u, h] = jnp.sum(weights, 0, keepdims=True)
        packed = weights.astype(jnp.bfloat16)
        if width > count:
            packed = jnp.concatenate([packed, jnp.zeros((width - count, width), jnp.bfloat16)], 0)
        rounded[u, h] = packed
    parts = {}
    for u, h in pairs:
        values = both[features + h * size : features + (h + 1) * size, u * width : (u + 1) * width]
        parts[u, h] = (dot(values, rounded[u, h]) * (1.0 / total[u, h])).astype(jnp.bfloat16)
    context = [jnp.concatenate([parts[u, h] for h in range(heads)], 0) for u in range(lines)]
    return dot(jnp.concatenate(context, 1), out_w, TN)


def lon_kernel(factor_ref, place_ref, *refs, blocks, bands, count, sizes):
    pieces = refs[:blocks]
    gain_ref, wk_ref, wqv_ref, wo_ref = refs[blocks : blocks + 4]
    *o_refs, state, normed, diag = refs[blocks + 4 :]
    part_cols, rows, features = pieces[0].shape
    cols = blocks * part_cols
    heads = factor_ref.shape[0]
    width = padded(cols, LANES)
    diag[...] = jnp.zeros_like(diag)
    lanes = [slice(c, c + LANES) for c in range(0, features, LANES)]
    for k, piece in enumerate(pieces):
        source = lax.rem(place_ref[0] + (blocks - k), blocks)
        x = piece[...].astype(jnp.float32).reshape(part_cols * rows, features)
        y = layer_norm(x, gain_ref[...])
        at = pl.ds(pl.multiple_of(source * (part_cols * rows), 8), part_cols * rows)
        for c, part in enumerate(lanes):
            state[c, at, :] = x[:, part]
            normed[c, at, :] = y[:, part]

    factors = [factor_ref[h] for h in range(heads)]

    unroll = diag.shape[0] * diag.shape[2] // (heads * width)

    @pl.loop(0, count // unroll)
    def _(group):
        spots = [pl.ds(group * unroll + u, cols, stride=rows) for u in range(unroll)]
        lines = []
        for at in spots:
            line = [normed.at[c][at, :].astype(jnp.bfloat16) for c in range(len(lanes))]
            line = jnp.concatenate(line, 1)
            if width > cols:
                line = jnp.concatenate([line, jnp.zeros((width - cols, features), jnp.bfloat16)], 0)
            lines.append(line)
        stack = jnp.concatenate(lines, 0)
        keys = dot(stack, wk_ref[...]).astype(jnp.bfloat16)
        both = dot(wqv_ref[...], stack, NT).astype(jnp.bfloat16)
        mixes = attend_lines(keys, both, factors, diag, wo_ref[...], cols, width, unroll)
        for u, at in enumerate(spots):
            mix = mixes[u * width : u * width + cols].astype(jnp.bfloat16).astype(jnp.float32)
            for c, part in enumerate(lanes):
                state.at[c][at, :] = state.at[c][at, :] + mix[:, part]

    for k, o_ref in enumerate(o_refs):
        target = lax.rem(place_ref[0] + k, blocks)
        at_out = 0
        for i in range(bands):
            near = i * sizes[0] + (0 if i < bands // 2 else part_cols - bands * sizes[0])
            for first, size in ((near, sizes[0]), (bands // 2 * sizes[0] + i * sizes[1], sizes[1])):
                start = (target * part_cols + first) * rows
                at = pl.ds(pl.multiple_of(start, 8), size * rows)
                y = jnp.concatenate([state[c, at, :] for c in range(len(lanes))], 1)
                y = y.reshape(size, rows, features).astype(jnp.bfloat16)
                o_ref[at_out : at_out + size] = y
                at_out += size


def lat_kernel(factor_ref, place_ref, *refs, bands, offset):
    count = len(refs) - bands - 7
    inputs = refs[:count]
    gain_ref, wk_ref, wqv_ref, wo_ref = refs[count : count + 4]
    *o_refs, line_ref, state, diag = refs[count + 4 :]
    blocks, _, rows, features = inputs[0].shape
    length = line_ref.shape[1]
    heads = factor_ref.shape[0]
    band = length // bands
    tall = o_refs[0].shape[1]

    @pl.when(pl.program_id(0) == 0)
    def _():
        diag[...] = jnp.zeros_like(diag)
        state[...] = jnp.zeros_like(state)

    cols = range(o_refs[0].shape[0])
    for n, x_ref in enumerate(inputs):
        source = lax.rem(place_ref[0] + (bands - n % bands), bands) if count > 1 else 0
        for m in range(blocks):
            block = lax.rem(place_ref[1] + (blocks - m), blocks) if count > 1 else 0
            start = source * band + block * (band // blocks) + n // bands * rows
            for u in cols:
                line_ref[u, pl.ds(pl.multiple_of(start, 8), rows), :] = x_ref[m, offset + u].astype(jnp.float32)
    lines = [layer_norm(line_ref[u], gain_ref[...]).astype(jnp.bfloat16) for u in cols]
    keys = [dot(line, wk_ref[...]).astype(jnp.bfloat16) for line in lines]
    both = [dot(wqv_ref[...], line, NT).astype(jnp.bfloat16) for line in lines]
    factors = [factor_ref[h] for h in range(heads)]
    mixes = attend_columns(keys, both, factors, diag, wo_ref[...])
    for u in cols:
        mix = mixes[u].astype(jnp.bfloat16).astype(jnp.float32)
        state[u, MARGIN : MARGIN + length, :] = line_ref[u] + mix
    for k, o_ref in enumerate(o_refs):
        target = lax.rem(place_ref[0] + k, bands)
        at = pl.ds(pl.multiple_of(target * band, 8), tall)
        for u in cols:
            o_ref[u] = state[u, at, :].astype(jnp.bfloat16)


def edge_column(source, count, bands, cols):
    return source * count + jnp.where(source < bands // 2, 0, cols - bands * count)


def mixer_kernel(place_ref, *refs, kinds, outs, filled, tile):
    inputs = refs[: len(kinds)]
    taps_ref, gain_ref, win_ref, wdown_ref = refs[len(kinds) : len(kinds) + 4]
    o_ref, wide, normed, done, sems = refs[len(kinds) + 4 + filled :]
    cols, rows, features = o_ref.shape
    hidden_len = wdown_ref.shape[0]
    bands = sum(kind == "near" for kind, _ in kinds)
    near_count = inputs[0].shape[0]
    for (kind, k), piece in zip(kinds, inputs):
        count = piece.shape[0]
        source = lax.rem(place_ref[0] + (bands - k), bands) if kind != "fixed" else 0
        if kind == "near":
            column = edge_column(source, count, bands, cols)
        elif kind == "far":
            column = bands // 2 * near_count + source * count
        else:
            column = k
        wide[pl.ds(column + MARGIN, count)] = piece[...].astype(jnp.float32)

    def smooth(n):
        source = outs[n]
        total = None
        for dy in range(KERNEL):
            part = None
            for dx in range(KERNEL):
                tap = taps_ref[dy * KERNEL + dx : dy * KERNEL + dx + 1, :]
                term = wide[source + dx] * tap
                part = term if part is None else part + term
            part = part[dy : dy + rows]
            total = part if total is None else total + part
        normed[n * rows : (n + 1) * rows, :] = layer_norm(total, gain_ref[...]).astype(jnp.bfloat16)

    def raise_up(t, k):
        line = normed[t * tile * rows : (t + 1) * tile * rows, :]
        gate = dot(line, win_ref[:, k])
        up = dot(line, win_ref[:, slice(hidden_len + k.start, hidden_len + k.stop)])
        return gate, up

    def bring_down(pair, k):
        gate, up = pair
        hidden = (0.5 * gate * (1.0 + jnp.tanh(0.5 * gate)) * up).astype(jnp.bfloat16)
        return dot(hidden, wdown_ref[k, :])

    for n in range(tile):
        smooth(n)
    chunk = hidden_len // tile
    copies = []
    for t in range(len(outs) // tile):
        update = None
        keys = [slice(n * chunk, (n + 1) * chunk) for n in range(tile)]
        pair = raise_up(t, keys[0])
        for n in range(tile):
            after = raise_up(t, keys[n + 1]) if n + 1 < tile else None
            if (t + 1) * tile + n < len(outs):
                smooth((t + 1) * tile + n)
            term = bring_down(pair, keys[n])
            pair = after
            update = term if update is None else update + term
        for n in range(tile):
            target = outs[t * tile + n]
            kept = wide[target + MARGIN, MARGIN : MARGIN + rows, :]
            done[t * tile + n] = (kept + update[n * rows : (n + 1) * rows]).astype(jnp.bfloat16)
            copies.append(
                pltpu.make_async_copy(done.at[t * tile + n], o_ref.at[target], sems.at[t * tile + n])
            )
            copies[-1].start()
    for copy in copies:
        copy.wait()


def whole(shape):
    return pl.BlockSpec(shape, lambda *_: (0,) * len(shape))


def split_weights(qkv, features):
    keys = qkv[:, features : 2 * features]
    both = jnp.concatenate([qkv[:, :features], qkv[:, 2 * features :]], 1).T
    return keys, both


SMEM = pl.BlockSpec(memory_space=pltpu.SMEM)
VMEM = pl.BlockSpec(memory_space=pltpu.VMEM)


def cost(cells, length, features, heads):
    return pl.CostEstimate(
        flops=2 * cells * features * (4 * features + (heads + 2) * length),
        bytes_accessed=4 * cells * features,
        transcendentals=cells * length * heads,
    )


def params(*sizes):
    return pltpu.CompilerParams(vmem_limit_bytes=min(60 * 2**20, 2 * sum(sizes) + 2**22))


def lon_call(pieces, place, factors, gains, weights, out_w, bands, count, sizes):
    blocks = len(pieces)
    part_cols, rows, features = pieces[0].shape
    all_cols = blocks * part_cols
    heads = factors.shape[0]
    unroll = next(u for u in (8, 2, 1) if u == 1 or (count % u == 0 and all_cols <= 2 * LANES))
    return pl.pallas_call(
        functools.partial(lon_kernel, blocks=blocks, bands=bands, count=count, sizes=sizes),
        out_shape=[jax.ShapeDtypeStruct((part_cols, rows, features), jnp.bfloat16)] * blocks,
        in_specs=[SMEM] * 2 + [VMEM] * (blocks + 4),
        out_specs=[VMEM] * blocks,
        scratch_shapes=[
            pltpu.VMEM((features // LANES, all_cols * rows, LANES), jnp.float32),
            pltpu.VMEM((features // LANES, all_cols * rows, LANES), jnp.float32),
            pltpu.VMEM((heads * unroll // 2, features, 2 * padded(all_cols, LANES)), jnp.bfloat16),
        ],
        cost_estimate=cost(all_cols * count, all_cols, features, heads),
        compiler_params=params(
            8 * all_cols * rows * features,
            2 * heads * unroll * features * padded(all_cols, LANES),
            4 * heads * unroll * all_cols * padded(all_cols, LANES),
        ),
        name="lon_attention",
    )(factors, place, *pieces, gains, *weights, out_w)


def lat_call(columns, first, count, place, factors, gains, weights, out_w, bands):
    blocks, _, rows, features = columns[0].shape
    heads = factors.shape[0]
    length = len(columns) * blocks * rows
    tall = padded(length // bands + 2 * MARGIN, 8)
    per = next(n for n in (2, 3, 1) if count % n == 0)
    offset = first if per == count else 0
    held = columns[0].shape[1] if per == count else per
    return pl.pallas_call(
        functools.partial(lat_kernel, bands=bands, offset=offset),
        grid=(count // per,),
        out_shape=[jax.ShapeDtypeStruct((count, tall, features), jnp.bfloat16)] * bands,
        in_specs=[
            SMEM,
            SMEM,
            *[pl.BlockSpec((blocks, held, rows, features), lambda k: (0, k + (first - offset) // per, 0, 0))]
            * len(columns),
            whole((1, features)),
            whole((features, features)),
            whole((2 * features, features)),
            whole((features, features)),
        ],
        out_specs=[pl.BlockSpec((per, tall, features), lambda k: (k, 0, 0))] * bands,
        scratch_shapes=[
            pltpu.VMEM((per, length, features), jnp.float32),
            pltpu.VMEM((per, length - length // bands + tall, features), jnp.float32),
            pltpu.VMEM((per, heads // 2, features, 2 * length), jnp.bfloat16),
        ],
        cost_estimate=cost(count * length, length, features, heads),
        compiler_params=params(
            12 * per * length * features,
            2 * per * heads * features * length,
            4 * heads * length * length,
        ),
        name="lat_attention",
    )(factors, place, *columns, gains, *weights, out_w)


def mixer_call(place, near, far, fixed, outs, cols, rows, out, taps, gains, win, wdown):
    inputs = [*near, *far, *[piece for _, piece in fixed]]
    kinds = [("near", k) for k in range(len(near))] + [("far", k) for k in range(len(far))]
    kinds += [("fixed", column) for column, _ in fixed]
    _, tall, features = inputs[0].shape
    count = len(outs)
    tile = next(n for n in (4, 2, 1) if count % n == 0)
    some = pl.BlockSpec(memory_space=pl.ANY)
    before = [] if out is None else [out]
    return pl.pallas_call(
        functools.partial(mixer_kernel, kinds=kinds, outs=outs, filled=len(before), tile=tile),
        out_shape=jax.ShapeDtypeStruct((cols, rows, features), jnp.bfloat16),
        in_specs=[SMEM] + [VMEM] * (len(inputs) + 4) + [some] * len(before),
        out_specs=some,
        scratch_shapes=[
            pltpu.VMEM((cols + 2 * MARGIN, tall, features), jnp.float32),
            pltpu.VMEM((count * rows, features), jnp.bfloat16),
            pltpu.VMEM((count, rows, features), jnp.bfloat16),
            pltpu.SemaphoreType.DMA((count,)),
        ],
        input_output_aliases={len(inputs) + 5: 0} if before else {},
        cost_estimate=pl.CostEstimate(
            flops=2 * count * rows * features * 3 * wdown.shape[0],
            bytes_accessed=4 * count * rows * features,
            transcendentals=count * rows * wdown.shape[0],
        ),
        compiler_params=params(
            4 * (cols + 2 * MARGIN) * tall * features, 8 * tile * rows * wdown.shape[0]
        ),
        name="mixer",
    )(place, *inputs, taps, gains, win, wdown, *before)


def per_device(
    fields,
    norm_gains,
    lon_qkv,
    lon_out,
    lat_qkv,
    lat_out,
    logit_scales,
    conv_taps,
    mlp_in,
    mlp_down,
):
    lat_rows, lon_cols, features = fields.shape
    blocks = lax.axis_size("lon")
    bands = lax.axis_size("lat")
    sub_rows = lat_rows // blocks
    tall_rows = padded(sub_rows, 8)
    sub_cols = lon_cols // bands
    factors = logit_scales * LOG2E

    grid = jnp.transpose(fields, (1, 0, 2)).reshape(lon_cols, blocks, sub_rows, features)
    if tall_rows > sub_rows:
        grid = jnp.pad(grid, ((0, 0), (0, 0), (0, tall_rows - sub_rows), (0, 0)))
    grid = grid.reshape(lon_cols, blocks * tall_rows, features)
    place = lax.axis_index("lon").astype(jnp.int32)
    band = lax.axis_index("lat").astype(jnp.int32)
    chunks = tall_rows // 8
    sizes = [sub_cols - sub_cols // 2, sub_cols // 2]
    weights = split_weights(lon_qkv, features)
    def along(pieces, axis, count):
        return [
            lax.ppermute(piece, axis, [(i, (i + k) % count) for i in range(count)]) if k else piece
            for k, piece in enumerate(pieces)
        ]

    moved = []
    for chunk in range(chunks):
        pieces = []
        for k in range(blocks):
            target = lax.rem(place + k, blocks)
            pieces.append(lax.dynamic_slice_in_dim(grid, target * tall_rows + chunk * 8, 8, 1))
        grid, pieces = lax.optimization_barrier((grid, pieces))
        moved.append(along(pieces, "lon", blocks))
    columns = []
    for chunk, pieces in enumerate(moved):
        count = min(8, sub_rows - chunk * 8)
        pieces = lon_call(
            pieces,
            place.reshape(1),
            factors[0],
            norm_gains[0:1],
            weights,
            lon_out,
            bands,
            count,
            sizes,
        )
        pieces = along(pieces, "lon", blocks)
        parts = []
        for k in range(bands):
            target = lax.rem(band + k, bands)
            parts.append(
                jnp.stack([lax.dynamic_slice_in_dim(p, target * sub_cols, sub_cols, 0) for p in pieces])
            )
        columns += along(parts, "lat", bands)
    if tall_rows > sub_rows:
        order = lax.rem(place + blocks - jnp.arange(blocks), blocks)
        columns = [
            jnp.swapaxes(jnp.take(part, order, 0)[:, :, :sub_rows], 0, 1).reshape(
                1, sub_cols, lat_rows, features
            )
            for part in columns
        ]
        order = lax.rem(band + bands - jnp.arange(bands), bands)
        columns = jnp.take(jnp.concatenate(columns), order, 0)
        columns = [jnp.swapaxes(columns, 0, 1).reshape(1, sub_cols, lat_rows * bands, features)]

    weights = split_weights(lat_qkv, features)

    def attend(first, count):
        spot = jnp.stack([band, place])
        return lat_call(
            columns, first, count, spot, factors[1], norm_gains[1:2], weights, lat_out, bands
        )

    near = along(attend(0, sizes[0]), "lat", bands)
    near, far = lax.optimization_barrier((near, attend(sizes[0], sizes[1])))
    far = along(far, "lat", bands)

    def pick(k, start, stop):
        chosen = near[0][start:stop]
        for n in range(1, bands):
            chosen = jnp.where(k == n, near[n][start:stop], chosen)
        return chosen

    up = [(i, (i + 1) % blocks) for i in range(blocks)]
    first = pick(band, 0, MARGIN)
    last = pick(lax.rem(band + 1, bands), sizes[0] - MARGIN, sizes[0])
    fixed = [
        (-MARGIN, lax.ppermute(last, "lon", up)),
        (lon_cols, lax.ppermute(first, "lon", [(j, i) for i, j in up])),
    ]
    mixer = (conv_taps, norm_gains[2:3], mlp_in, mlp_down)
    side = bands // 2 * sizes[0]
    ready = [*range(MARGIN, side - MARGIN), *range(lon_cols - side + MARGIN, lon_cols - MARGIN)]
    late = [c for c in range(lon_cols) if c not in ready]
    spot = band.reshape(1)
    out = mixer_call(spot, near, [], [], ready, lon_cols, lat_rows, None, *mixer)
    out = mixer_call(spot, near, far, fixed, late, lon_cols, lat_rows, out, *mixer)
    return jnp.transpose(out, (1, 0, 2))


def solution(mesh):
    in_specs = (P(("groups", "lat"), "lon", None), P(), P(), P(), P(), P(), P(), P(), P(), P())
    out_specs = P(("groups", "lat"), "lon", None)
    return jax.shard_map(
        per_device, mesh=mesh, in_specs=in_specs, out_specs=out_specs, check_vma=False
    )
```
